512 devices in a mesh: dp: 16 (over x_hi, y), mp: 32 (over z, x_lo, core).
Axes of the slice: x: 4 (x_hi: 2, x_lo: 2; x = x_hi * 2 + x_lo), y: 8, z: 8, core: 2. Of those that a mesh axis runs over, the one named last changes fastest.
Arguments:
- frames: bfloat16 [4096, 1536], P('dp', 'mp'), may hold values from -6 to 6
- conv_kernel: bfloat16 [32, 1536], P(None, 'mp'), may hold values from -1 to 1
- head_weight: bfloat16 [1536, 16384], P(None, 'mp'), may hold values from -13 to 13
- utterance_ids: int32 [16, 256], P('dp'), may hold values from 0 to 3, never falling along the last dimension, each value on 1 to 128 neighbouring positions
- tile_used: int32 [16], P('dp'), may hold values from 128 to 256
- teacher_ids: int32 [4096, 32], P('dp'), may hold values from 0 to 16383, all different within a row
- teacher_logits: int32 [4096, 32], P('dp'), may hold values from -127 to 127
- teacher_scale: float32 [4096], P('dp'), may hold values from 0.03 to 3
Outputs:
- input_grad: float32 [4096, 1536], P('dp', 'mp')
- kernel_grad: float32 [32, 1536], P(None, 'mp')
- head_grad: float32 [1536, 16384], P('dp', 'mp')
The draws below stay inside these ranges and needn't reach their ends.
All inputs are finite; a program needn't handle non-finite values.
Results may differ from the reference program's by a relative error of at most 0.02.
The reference program's roundings to bfloat16 on the way (of `conv` and `logit_grad`) count: a program that leaves them out, or rounds other values in their place, can miss the bound.
Values may be sent and summed in bfloat16 or wider, within the bound.
A program may use at most 64 MiB of HBM per device.

```python
import math
import jax
import jax.numpy as jnp
import numpy as np
from jax import lax

D = 1536
VOCAB = 16384
KERNEL = 32
TOP = 32
TILE = 256
TILES = 16
FRAMES = 4096
N_MP = 32


def draw_head_weight(key, part):
    first = jax.random.fold_in(key, 0)
    weight = jax.random.truncated_normal(first, -4.0, 4.0, (D, VOCAB), jnp.float32) * (3.0 / math.sqrt(D))
    return weight.astype(jnp.bfloat16)


def draw_tile_used(key, part):
    used = TILE - jax.random.randint(key, (TILES,), 0, TILE // 2 + 1)
    used = used.at[0].set(TILE).at[1].set(TILE - TILE // 2)
    return used.astype(jnp.int32)


def draw_teacher_scale(key, part):
    upper = math.log(0.15)
    return jnp.exp(jax.random.uniform(key, (FRAMES,), jnp.float32, math.log(0.03), upper))


def set_ends(values, key, smallest, high):
    longest = values.shape.index(max(values.shape))
    spots = []
    for shift in (0, 1):
        where = [jax.random.randint(jax.random.fold_in(key, axis), (), 0, length) for axis, length in enumerate(values.shape)]
        where[longest] = (where[longest] + shift) % values.shape[longest]
        spots.append(tuple(where))
    return values.at[spots[0]].set(smallest).at[spots[1]].set(high)


def block_scale(key, extent, shards, low, largest):
    factor_of = 1.0
    for position, parts in shards:
        draws = jax.random.uniform(jax.random.fold_in(jax.random.fold_in(key, 6), position), (parts,), jnp.float32, low / len(shards), largest / len(shards))
        factor_of = factor_of * jnp.repeat(jnp.exp(draws), extent[position] // parts).reshape((-1,) + (1,) * (len(extent) - 1 - position))
    return factor_of


def distinct(stream_key, rows, amount, top, lift):
    sequence = jax.random.permutation(jax.random.fold_in(stream_key, 1), amount)
    favour = sequence
    for power in range(3):
        favour = favour * favour // amount
    favour = favour * lift // amount
    chance = jax.random.randint(jax.random.fold_in(stream_key, 2), (rows, amount), 0, 4096) + favour
    fixed_rows = jax.random.permutation(jax.random.fold_in(stream_key, 3), rows)[jnp.arange(amount) % rows]
    chance = jnp.where(jnp.arange(rows)[:, None] == fixed_rows[None, :], 1 << 14, chance)
    priority = chance * amount + jnp.arange(amount)
    return lax.top_k(priority.astype(jnp.int32), top)[1].astype(jnp.int32)


def profile(count, total, bound, lean):
    loads = [(1 << 20) // math.isqrt(rank ** lean) + 1 for rank in range(2, count + 1)]
    surplus, counts = total - bound - (count - 1), [1] * (count - 1)
    while surplus > 0:
        free = [i for i in range(count - 1) if counts[i] < bound]
        whole, remaining = sum([loads[i] for i in free]), surplus
        for i in free:
            more = min(bound - counts[i], max(1, remaining * loads[i] // whole), surplus)
            counts[i] = counts[i] + more
            surplus = surplus - more
    return np.array([bound] + counts)


def uneven(own_key, amount, total, limit, skew):
    if amount == 2:
        one = jax.random.randint(own_key, (), max(1, total - limit), min(limit, total - 1) + 1)
        return jnp.stack([one, total - one])
    tallies = jnp.asarray(profile(amount, total, limit, skew), jnp.int32)
    couples = (amount - 1) // 2
    donor, receiver = tallies[1:1 + 2 * couples:2], tallies[2:2 + 2 * couples:2]
    slack = jnp.minimum(donor - 1, limit - receiver)
    passed = jax.random.randint(jax.random.fold_in(own_key, 1), (couples,), 0, 1 << 20) % (slack + 1)
    tallies = tallies.at[1:1 + 2 * couples:2].set(donor - passed).at[2:2 + 2 * couples:2].set(receiver + passed)
    return tallies[jax.random.permutation(jax.random.fold_in(own_key, 2), amount)]


def noise(stream_key, extent, scale, most, cuts=(), kind=jnp.bfloat16):
    drawn = scale * jax.random.normal(stream_key, extent, jnp.float32)
    if cuts:
        drawn = drawn * block_scale(stream_key, extent, cuts, -0.22, 0.18)
    return jnp.clip(drawn, -most, most).astype(kind)


def setup_inputs(seed: int = 0) -> dict:
    key_list = jax.random.split(jax.random.key(seed), 9)
    return {
        "frames": noise(key_list[0], (FRAMES, D), 1.0, 6.0, ((0, 16), (1, 32))),
        "conv_kernel": noise(key_list[1], (KERNEL, D), KERNEL ** -0.5, 1.0, ((1, 32),)),
        "head_weight": draw_head_weight(jax.random.fold_in(key_list[8], 71), 0),
        "utterance_ids": jax.vmap(lambda own: jnp.searchsorted(jnp.cumsum(uneven(own, max(4, TILE // 64), TILE, TILE // 2, 2)), jnp.arange(TILE), side="right"))(jax.random.split(key_list[3], TILES)).reshape((TILES, TILE)).astype(jnp.int32),
        "tile_used": draw_tile_used(jax.random.fold_in(key_list[8], 71), 0),
        "teacher_ids": distinct(key_list[5], FRAMES, VOCAB, TOP, 32),
        "teacher_logits": set_ends(jax.random.randint(key_list[6], (FRAMES, TOP), -127, 128), jax.random.fold_in(key_list[6], 1), -127, 127).astype(jnp.int32),
        "teacher_scale": draw_teacher_scale(jax.random.fold_in(key_list[8], 71), 0),
    }


def conv_tile(source, taps, seg_row, valid_row):
    count = source.shape[0]
    left = (KERNEL - 1) // 2
    right = KERNEL - 1 - left
    padded = jnp.pad(source, ((left, right), (0, 0)))
    seg_pad = jnp.pad(seg_row, (left, right), constant_values=-1)
    valid_pad = jnp.pad(valid_row, (left, right), constant_values=False)
    result = jnp.zeros(source.shape, jnp.float32)
    for tap in range(KERNEL):
        keep = (seg_pad[tap:tap + count] == seg_row) & valid_pad[tap:tap + count] & valid_row
        result = result + jnp.where(keep[:, None], padded[tap:tap + count] * taps[tap], 0.0)
    return result

def rounded(value):
    return lax.optimization_barrier(value.astype(jnp.bfloat16)).astype(jnp.float32)

def reference(frames, conv_kernel, head_weight, utterance_ids, tile_used, teacher_ids, teacher_logits, teacher_scale):
    width = frames.shape[1]
    block = VOCAB // N_MP
    kern = conv_kernel.astype(jnp.float32)
    weight_f = head_weight.astype(jnp.float32)
    weight_blocks = weight_f.reshape(width, N_MP, block).transpose(1, 0, 2)
    frames_t = frames.reshape(TILES, TILE, width)
    ids_t = teacher_ids.reshape(TILES, TILE, TOP)
    logit_t = teacher_logits.reshape(TILES, TILE, TOP)
    scale_t = teacher_scale.reshape(TILES, TILE)

    def step(carry, items):
        head_acc, kernel_acc = carry
        source, seg_row, used, ids_row, quant, scale = items
        valid = jnp.arange(TILE, dtype=jnp.int32) < used

        def convolve(values, taps):
            return conv_tile(values, taps, seg_row, valid)
        conv = convolve(source.astype(jnp.float32), kern).astype(jnp.bfloat16)
        conv_f = conv.astype(jnp.float32)
        logits = jnp.dot(conv_f, weight_f, preferred_element_type=jnp.float32)
        peak = lax.optimization_barrier(jnp.max(logits, axis=1))
        total = lax.optimization_barrier(jnp.sum(jnp.exp(logits - peak[:, None]), axis=1))
        normaliser = peak + jnp.log(total)
        teacher = jax.nn.softmax(scale[:, None] * quant.astype(jnp.float32), axis=1)
        rowpos = jnp.arange(TILE, dtype=jnp.int32)[:, None]
        target = jnp.zeros((TILE, VOCAB), jnp.float32).at[rowpos, ids_row].add(teacher)
        logit_grad = jnp.where(valid[:, None], jnp.exp(logits - normaliser[:, None]) - target, 0.0).astype(jnp.bfloat16)
        grad_f = logit_grad.astype(jnp.float32)
        head_part = rounded(jnp.dot(conv_f.T, grad_f, preferred_element_type=jnp.float32))
        grad_blocks = grad_f.reshape(TILE, N_MP, block).transpose(1, 0, 2)

        def add_block(acc, pair):
            grad_b, weight_b = pair
            return (acc + rounded(jnp.dot(grad_b, weight_b.T, preferred_element_type=jnp.float32)), None)
        conv_grad, _ = lax.scan(add_block, jnp.zeros((TILE, width), jnp.float32), (grad_blocks, weight_blocks))
        _, pull = jax.vjp(convolve, source.astype(jnp.float32), kern)
        input_part, kernel_part = pull(conv_grad)
        return ((head_acc + head_part, kernel_acc + kernel_part), input_part)
    start = (jnp.zeros((width, VOCAB), jnp.float32), jnp.zeros((KERNEL, width), jnp.float32))
    (head_grad, kernel_grad), input_parts = lax.scan(step, start, (frames_t, utterance_ids, tile_used, ids_t, logit_t, scale_t))
    return (input_parts.reshape(FRAMES, width), kernel_grad, head_grad)
```

```python
import functools

import jax
import jax.numpy as jnp
from jax import lax
from jax.experimental import pallas as pl
from jax.experimental.pallas import tpu as pltpu
from jax.sharding import PartitionSpec as P

MESH = pl.DeviceIdType.MESH
TAPS = 32
LEFT = (TAPS - 1) // 2
TOP = 32
NZ = 8
NY = 8
CH = 48
T = 256
VOC = 512
ZX = 16
F32 = jnp.float32
BF = jnp.bfloat16

NEAR = (1, 7, 2, 6, 3, 5, 4)
FAR = (4, 3, 5, 2, 6, 1, 7)


def eye(n):
    same = lax.broadcasted_iota(jnp.int32, (n, n), 0) == lax.broadcasted_iota(jnp.int32, (n, n), 1)
    return jnp.where(same, 1.0, 0.0).astype(BF)


def turned(values):
    return lax.dot_general(
        eye(values.shape[1]), values, (((1,), (1,)), ((), ())), preferred_element_type=F32
    )


def kernel(
    frames, taps, w_hbm, seg, used, ids, tlog, scale,
    out_in, out_k, out_h,
    w, wt, conv, xt, src_rows, dst_rows, rel_ids, teach, tgt, ex, stats, gt,
    cg, cin, xsend, xin, zsend, zin,
    hh, rin, xfin, xrin, kg, kx, ky,
    w_sem, a_send, a_recv, b_send, b_recv, dc_send, dc_recv, dx_send, dx_recv, dz_send, dz_recv,
    r_send, r_recv, cx_send, cx_recv, k_send, k_recv,
):
    m = lax.axis_index("mp")
    d = lax.axis_index("dp")
    c, xl, z = m % 2, (m // 2) % 2, m // 4
    y, xh = d % NY, d // NY
    zx = m // 2
    oc, ox, oh = 1 - c, 1 - xl, 1 - xh
    core_peer = {"mp": m + 1 - 2 * c}
    x_peer = {"mp": m + 2 - 4 * xl}
    h_peer = {"dp": oh * NY + y}

    def z_at(off):
        return (z + off) % NZ

    def z_peer(off):
        return {"mp": z_at(off) * 4 + xl * 2 + c}

    def y_at(off):
        return (y + off + NY) % NY

    def y_peer(off):
        return {"dp": xh * NY + y_at(off)}

    load_w = pltpu.make_async_copy(w_hbm, w, w_sem)
    load_w.start()

    barrier = pltpu.get_barrier_semaphore()

    @pl.loop(1, 32)
    def _(off):
        pl.semaphore_signal(barrier, inc=1, device_id={"mp": (m + off) % 32}, device_id_type=MESH)

    for off in range(1, NY):
        pl.semaphore_signal(barrier, inc=1, device_id=y_peer(off), device_id_type=MESH)
    pl.semaphore_signal(barrier, inc=1, device_id=h_peer, device_id_type=MESH)

    def remote(src, dst, send, recv, peer):
        return pltpu.make_async_remote_copy(
            src_ref=src, dst_ref=dst, send_sem=send, recv_sem=recv, device_id=peer, device_id_type=MESH
        )

    lane = lax.broadcasted_iota(jnp.int32, (8, T), 1)
    valid = lane < used[0]
    seg_rows = jnp.broadcast_to(seg[...], (8, T))
    src_rows[...] = jnp.where(valid, seg_rows, -1)
    dst_rows[...] = jnp.where(valid, seg_rows, -2)
    xt[...] = turned(frames[...])
    tap_t = turned(taps[...])

    def kept(delta):
        rolled = src_rows[...]
        if delta:
            rolled = pltpu.roll(rolled, (-delta) % T, 1)
        keep = rolled == dst_rows[...]
        if delta > 0:
            keep = keep & (lane < T - delta)
        if delta < 0:
            keep = keep & (lane >= -delta)
        return keep

    def moved(values, delta):
        return pltpu.roll(values, (-delta) % T, 1) if delta else values

    def only(keep, values):
        return jnp.where(keep[None], values.reshape(CH // 8, 8, T), 0.0).reshape(CH, T)

    acc = jnp.zeros((CH, T), F32)
    for j in range(TAPS):
        delta = j - LEFT
        acc = acc + only(kept(delta), moved(xt[...], delta) * tap_t[:, j : j + 1])
    conv[c, zx] = acc.astype(BF)

    pl.semaphore_wait(barrier, 31 + NY)

    def a_copy(slot_c, slot_zx, k, peer):
        return remote(
            conv.at[slot_c, slot_zx], conv.at[slot_c, slot_zx], a_send.at[k], a_recv.at[slot_c, slot_zx], peer
        )

    sent = []
    for k, off in enumerate(FAR):
        copy = a_copy(c, zx, k, z_peer(off))
        copy.start()
        sent.append(copy)
    copy = a_copy(c, zx, 7, x_peer)
    copy.start()
    sent.append(copy)
    copy = a_copy(c, zx, 8, core_peer)
    copy.start()
    sent.append(copy)

    load_w.wait()
    for half in range(2):
        for v in range(VOC // 128):
            part = w[:, half, :, v * 128 : (v + 1) * 128].reshape(ZX * CH, 128)
            wt[half, v * 128 : (v + 1) * 128, :] = part.T

    def teacher_work():
        upper = turned((ids[...] // 128).astype(F32).astype(BF))
        lower = turned((ids[...] % 128).astype(F32).astype(BF))
        rel_ids[...] = upper.astype(jnp.int32) * 128 + lower.astype(jnp.int32) - m * VOC
        scores = scale[...].reshape(1, T) * turned(tlog[...].astype(F32).astype(BF))
        top = jnp.exp(scores - jnp.max(scores, axis=0, keepdims=True))
        teach[...] = top / jnp.sum(top, axis=0, keepdims=True)

        @pl.loop(0, VOC // 64)
        def _(part):
            first = pl.multiple_of(part * 64, 64)
            row = lax.broadcasted_iota(jnp.int32, (64, T), 0) + first
            found = jnp.zeros((64, T), F32)
            for k in range(TOP):
                found = jnp.where(row == rel_ids[k : k + 1, :], teach[k : k + 1, :], found)
            tgt[pl.ds(first, 64), :] = found

    k = 9
    for off in NEAR:
        slot = z_at(off) * 2 + xl
        a_copy(c, slot, 0, z_peer(off)).wait_recv()
        for peer in (x_peer, core_peer):
            copy = a_copy(c, slot, k, peer)
            copy.start()
            sent.append(copy)
            k += 1
    teacher_work()
    for off in (0, *NEAR):
        slot = z_at(off) * 2 + ox
        a_copy(c, slot, 0, x_peer).wait_recv()
        copy = a_copy(c, slot, k, core_peer)
        copy.start()
        sent.append(copy)
        k += 1
    logits = jnp.dot(wt[c], conv[c].reshape(ZX * CH, T), preferred_element_type=F32)

    @pl.loop(0, ZX)
    def _(slot):
        a_copy(oc, slot, 0, core_peer).wait_recv()

    logits = logits + jnp.dot(wt[oc], conv[oc].reshape(ZX * CH, T), preferred_element_type=F32)

    peak = jnp.max(logits, axis=0, keepdims=True)
    raised = jnp.exp(logits - peak)
    ex[...] = raised
    own = peak + jnp.log(jnp.sum(raised, axis=0, keepdims=True))
    stats[m] = own

    def b_copy(off, slot):
        return remote(
            stats.at[slot], stats.at[slot], b_send.at[off], b_recv.at[slot], {"mp": (m + off) % 32}
        )

    @pl.loop(1, 32)
    def _(off):
        b_copy(off, m).start()

    for copy in sent:
        copy.wait_send()

    @pl.loop(1, 32)
    def _(off):
        b_copy(off, (m + off) % 32).wait_recv()

    every = stats[...]
    most = jnp.max(every, axis=0)
    norm = most + jnp.log(jnp.sum(jnp.exp(every - most[None]), axis=0))
    factor = jnp.exp(peak - norm)
    live = lax.broadcasted_iota(jnp.int32, (1, T), 1) < used[0]
    gt[...] = jnp.where(live, ex[...] * factor - tgt[...], 0.0).astype(BF)

    w_all = w[...].reshape(ZX * 2 * CH, VOC)
    cg[...] = (
        jnp.dot(w_all, gt[...], preferred_element_type=F32).astype(BF).reshape(NZ, 2, 2, CH, T)
    )
    core_copies = []
    for k, side in enumerate((ox, xl)):
        copy = remote(cg.at[:, side, oc], cin.at[k], dc_send.at[k], dc_recv.at[k], core_peer)
        copy.start()
        core_copies.append(copy)

    for half in range(2):
        hh[half] = (
            lax.dot_general(
                conv[half].reshape(ZX * CH, T), gt[...], (((1,), (1,)), ((), ())), preferred_element_type=F32
            )
            .astype(BF)
            .reshape(ZX, CH, VOC)
        )

    def r_copy(way, dist, half, side, owner):
        row = (oh if side == 0 else xh) * NY + owner
        return remote(
            hh.at[half, row],
            rin.at[way, dist - 1, half, side],
            r_send.at[way, dist - 1, half, side],
            r_recv.at[way, dist - 1, half, side],
            y_peer(1 if way else -1),
        )

    def r_step(dist, late):
        for side in range(2):
            for way in range(2):
                toward = dist if way else -dist
                owner = y_at(toward)
                if dist == 4:
                    half = way
                    r_copy(way, dist, half, side, owner).start()
                    continue
                half = way if late else 1 - way
                row = (oh if side == 0 else xh) * NY + owner
                if dist < 3 or late:
                    r_copy(way, dist + 1, half, side, owner).wait_recv()
                    hh[half, row] = (
                        hh[half, row].astype(F32) + rin[way, dist, half, side].astype(F32)
                    ).astype(BF)
                r_copy(way, dist, half, side, owner).start()

    r_step(4, True)
    r_step(3, False)

    def dx_copy(slot):
        return remote(xsend.at[slot], xin.at[slot], dx_send.at[slot], dx_recv.at[slot], x_peer)

    core_copies[0].wait_recv()
    for off in (*FAR, 0):
        at = z_at(off)
        xsend[at] = (cg[at, ox, c].astype(F32) + cin[0, at].astype(F32)).astype(BF)
        dx_copy(at).start()
    core_copies[1].wait_recv()

    def dz_copy(off, slot):
        return remote(zsend.at[slot], zin.at[off], dz_send.at[off], dz_recv.at[off], z_peer(off))

    def d_step(off):
        at = z_at(off)
        dx_copy(at).wait_recv()
        total = cg[at, xl, c].astype(F32) + cin[1, at].astype(F32) + xin[at].astype(F32)
        if off == 0:
            return total
        zsend[at] = total.astype(BF)
        dz_copy(off, at).start()

    for off in FAR[:4]:
        d_step(off)
    r_step(3, True)
    for off in FAR[4:]:
        d_step(off)
    conv_grad = d_step(0)
    r_step(2, False)
    r_step(2, True)
    for off in FAR:
        dz_copy(off, z_at(off)).wait_recv()
        conv_grad = conv_grad + zin[off].astype(F32)

    group = lax.broadcasted_iota(jnp.int32, (1, 8, 128), 2)
    packed = jnp.zeros((2, 8, 128), F32)
    for j in range(TAPS):
        delta = j - LEFT
        terms = moved(xt[...], delta) * only(kept(delta), conv_grad)
        sums = jnp.sum(terms, axis=1, keepdims=True).reshape(CH // 8, 8, 1)
        for g in range(3):
            packed = jnp.where(group == g * TAPS + j, sums[2 * g : 2 * g + 2], packed)
    kg[...] = packed.reshape(16, 128)
    k_over = remote(kg, kx, k_send.at[0], k_recv.at[0], h_peer)
    k_over.start()

    r_step(1, False)

    acc = jnp.zeros((CH, T), F32)
    for j in range(TAPS):
        delta = j - LEFT
        acc = acc + moved(only(kept(delta), conv_grad) * tap_t[:, j : j + 1], -delta)
    out_in[...] = acc

    k_over.wait_recv()
    ky[y] = kg[...] + kx[...]

    def k_copy(off, slot):
        return remote(ky.at[slot], ky.at[slot], k_send.at[off], k_recv.at[slot + 1], y_peer(off))

    for off in range(1, NY):
        k_copy(off, y).start()

    r_step(1, True)

    def cx_copy(half):
        return remote(xfin.at[half], xrin.at[half], cx_send.at[half], cx_recv.at[half], h_peer)

    def y_total(half, side):
        row = (oh if side == 0 else xh) * NY + y
        total = hh[half, row].astype(F32)
        for way in range(2):
            r_copy(way, 1, half, side, y).wait_recv()
            total = total + rin[way, 0, half, side].astype(F32)
        return total

    for half in range(2):
        xfin[half] = y_total(half, 0).astype(BF)
        cx_copy(half).start()

    for off in range(1, NY):
        k_copy(off, y_at(off)).wait_recv()
    out_k[...] = jnp.sum(ky[...], axis=0)

    for half in range(2):
        total = y_total(half, 1)
        cx_copy(half).wait_recv()
        out_h[half] = total + xrin[half].astype(F32)

    @pl.loop(1, 32)
    def _(off):
        b_copy(off, m).wait_send()

    for copy in core_copies:
        copy.wait_send()
    for off in (*FAR, 0):
        dx_copy(z_at(off)).wait_send()
    for off in FAR:
        dz_copy(off, z_at(off)).wait_send()
    for way in range(2):
        for side in range(2):
            r_copy(way, 4, way, side, y).wait_send()
            for dist in range(1, 4):
                for half in range(2):
                    r_copy(way, dist, half, side, y).wait_send()
    for half in range(2):
        cx_copy(half).wait_send()
    k_over.wait_send()
    for off in range(1, NY):
        k_copy(off, y).wait_send()


def local(frames, conv_kernel, head_weight, utterance_ids, tile_used, teacher_ids, teacher_logits, teacher_scale):
    vmem = pl.BlockSpec(memory_space=pltpu.VMEM)
    dma = pltpu.SemaphoreType.DMA
    grad, packed, head = pl.pallas_call(
        kernel,
        out_shape=(
            jax.ShapeDtypeStruct((CH, T), F32),
            jax.ShapeDtypeStruct((16, 128), F32),
            jax.ShapeDtypeStruct((2, CH, VOC), F32),
        ),
        in_specs=[
            vmem,
            vmem,
            pl.BlockSpec(memory_space=pl.ANY),
            vmem,
            pl.BlockSpec(memory_space=pltpu.SMEM),
            vmem,
            vmem,
            vmem,
        ],
        out_specs=(vmem, vmem, vmem),
        scratch_shapes=[
            pltpu.VMEM((ZX, 2, CH, VOC), BF),
            pltpu.VMEM((2, VOC, ZX * CH), BF),
            pltpu.VMEM((2, ZX, CH, T), BF),
            pltpu.VMEM((CH, T), F32),
            pltpu.VMEM((8, T), jnp.int32),
            pltpu.VMEM((8, T), jnp.int32),
            pltpu.VMEM((TOP, T), jnp.int32),
            pltpu.VMEM((TOP, T), F32),
            pltpu.VMEM((VOC, T), F32),
            pltpu.VMEM((VOC, T), F32),
            pltpu.VMEM((32, 1, T), F32),
            pltpu.VMEM((VOC, T), BF),
            pltpu.VMEM((NZ, 2, 2, CH, T), BF),
            pltpu.VMEM((2, NZ, CH, T), BF),
            pltpu.VMEM((NZ, CH, T), BF),
            pltpu.VMEM((NZ, CH, T), BF),
            pltpu.VMEM((NZ, CH, T), BF),
            pltpu.VMEM((NZ, CH, T), BF),
            pltpu.VMEM((2, ZX, CH, VOC), BF),
            pltpu.VMEM((2, 4, 2, 2, CH, VOC), BF),
            pltpu.VMEM((2, CH, VOC), BF),
            pltpu.VMEM((2, CH, VOC), BF),
            pltpu.VMEM((16, 128), F32),
            pltpu.VMEM((16, 128), F32),
            pltpu.VMEM((NY, 16, 128), F32),
            dma,
            dma((32,)),
            dma((2, ZX)),
            dma((32,)),
            dma((32,)),
            dma((2,)),
            dma((2,)),
            dma((NZ,)),
            dma((NZ,)),
            dma((NZ,)),
            dma((NZ,)),
            dma((2, 4, 2, 2)),
            dma((2, 4, 2, 2)),
            dma((2,)),
            dma((2,)),
            dma((NY,)),
            dma((NY + 1,)),
        ],
        compiler_params=pltpu.CompilerParams(
            collective_id=0, has_side_effects=True, vmem_limit_bytes=56 * 1024 * 1024
        ),
    )(
        frames,
        conv_kernel,
        head_weight.reshape(ZX, 2, CH, VOC),
        utterance_ids,
        tile_used,
        teacher_ids,
        teacher_logits,
        teacher_scale,
    )
    kernel_grad = packed[:, : 3 * TAPS].reshape(16, 3, TAPS).transpose(2, 1, 0).reshape(TAPS, CH)
    return grad.T, kernel_grad, head.reshape(2 * CH, VOC)


def solution(mesh):
    return jax.shard_map(
        local,
        mesh=mesh,
        in_specs=(
            P("dp", "mp"),
            P(None, "mp"),
            P(None, "mp"),
            P("dp", None),
            P("dp"),
            P("dp", None),
            P("dp", None),
            P("dp"),
        ),
        out_specs=(P("dp", "mp"), P(None, "mp"), P("dp", "mp")),
        check_vma=False,
    )
```

```python
import jax
import jax.numpy as jnp
from jax import lax
from jax.experimental import pallas as pl
from jax.experimental.pallas import tpu as pltpu
from jax.sharding import PartitionSpec as P

MESH = pl.DeviceIdType.MESH
TAPS = 32
LEFT = (TAPS - 1) // 2
TOP = 32
NZ = 8
NY = 8
CH = 48
T = 256
VOC = 512
ZX = 16
F32 = jnp.float32
BF = jnp.bfloat16

NEAR = (1, 7, 2, 6, 3, 5, 4)
FAR = (4, 3, 5, 2, 6, 1, 7)
SENDS = (4, 1, 7, 2, 6, 3, 5)


def eye(n):
    same = lax.broadcasted_iota(jnp.int32, (n, n), 0) == lax.broadcasted_iota(jnp.int32, (n, n), 1)
    return jnp.where(same, 1.0, 0.0).astype(BF)


def turned(values):
    return lax.dot_general(
        eye(values.shape[1]), values, (((1,), (1,)), ((), ())), preferred_element_type=F32
    )


def kernel(
    used, frames_hbm, taps_hbm, w_hbm, seg_hbm, ids_hbm, tlog_hbm, scale_hbm,
    out_in, out_k, out_h,
    frames, taps, seg, ids, tlog, scale,
    w, wt, conv, xt, xm, src_rows, dst_rows, rel_ids, teach, tgt, ex, stats, gt,
    cg, cin, xsend, xin, zsend, zin, grad,
    hh, rin, xfin, xrin, ky,
    in_sem, a_send, a_recv, b_send, b_recv, dc_send, dc_recv, dx_send, dx_recv, dz_send, dz_recv,
    r_send, r_recv, cx_send, cx_recv, k_send, k_recv,
):
    m = lax.axis_index("mp")
    d = lax.axis_index("dp")
    c, xl, z = m % 2, (m // 2) % 2, m // 4
    y, xh = d % NY, d // NY
    zx = m // 2
    oc, ox, oh = 1 - c, 1 - xl, 1 - xh
    core_peer = {"mp": m + 1 - 2 * c}
    x_peer = {"mp": m + 2 - 4 * xl}
    h_peer = {"dp": oh * NY + y}

    def z_at(off):
        return (z + off) % NZ

    def z_peer(off):
        return {"mp": z_at(off) * 4 + xl * 2 + c}

    def y_at(off):
        return (y + off + NY) % NY

    def y_peer(off):
        return {"dp": xh * NY + y_at(off)}

    pairs = (
        (frames_hbm, frames), (taps_hbm, taps), (seg_hbm, seg),
        (w_hbm, w), (ids_hbm, ids), (tlog_hbm, tlog), (scale_hbm, scale),
    )
    loads = [pltpu.make_async_copy(src, dst, in_sem.at[k]) for k, (src, dst) in enumerate(pairs)]
    for load in loads:
        load.start()

    barrier = pltpu.get_barrier_semaphore()

    @pl.loop(1, 32)
    def _(off):
        pl.semaphore_signal(barrier, inc=1, device_id={"mp": (m + off) % 32}, device_id_type=MESH)

    @pl.loop(1, 16)
    def _(off):
        pl.semaphore_signal(barrier, inc=1, device_id={"dp": (d + off) % 16}, device_id_type=MESH)

    def remote(src, dst, send, recv, peer):
        return pltpu.make_async_remote_copy(
            src_ref=src, dst_ref=dst, send_sem=send, recv_sem=recv, device_id=peer, device_id_type=MESH
        )

    for load in loads[:3]:
        load.wait()

    lane = lax.broadcasted_iota(jnp.int32, (8, T), 1)
    valid = lane < used[0]
    seg_rows = jnp.broadcast_to(seg[...], (8, T))
    src_rows[...] = jnp.where(valid, seg_rows, -1)
    dst_rows[...] = jnp.where(valid, seg_rows, -2)
    xt[...] = frames[...].astype(F32)
    tap_t = turned(taps[...])

    def kept(delta):
        rolled = src_rows[...]
        if delta:
            rolled = pltpu.roll(rolled, (-delta) % T, 1)
        keep = rolled == dst_rows[...]
        if delta > 0:
            keep = keep & (lane < T - delta)
        if delta < 0:
            keep = keep & (lane >= -delta)
        return keep

    def moved(values, delta):
        return pltpu.roll(values, (-delta) % T, 1) if delta else values

    def only(keep, values):
        return jnp.where(keep[None], values.reshape(CH // 8, 8, T), 0.0).reshape(CH, T)

    acc = jnp.zeros((CH, T), F32)
    for j in range(TAPS):
        delta = j - LEFT
        source = only(kept(delta), moved(xt[...], delta))
        xm[j] = source
        acc = acc + source * tap_t[:, j : j + 1]
    conv[c, zx] = acc.astype(BF)

    pl.semaphore_wait(barrier, 31 + 15)

    def a_copy(slot_c, slot_zx, k, peer):
        return remote(
            conv.at[slot_c, slot_zx], conv.at[slot_c, slot_zx], a_send.at[k], a_recv.at[slot_c, slot_zx], peer
        )

    sent = []

    def a_start(slot, peer):
        copy = a_copy(c, slot, len(sent), peer)
        copy.start()
        sent.append(copy)

    a_start(zx, x_peer)
    a_start(zx, core_peer)
    for off in SENDS:
        a_start(zx, z_peer(off))

    for load in loads[3:]:
        load.wait()
    for half in range(2):
        for v in range(VOC // 128):
            part = w[:, :, half, :, v * 128 : (v + 1) * 128].reshape(ZX * CH, 128)
            wt[half, v * 128 : (v + 1) * 128, :] = part.T

    rel_ids[...] = ids[...] - m * VOC
    scores = scale[...].reshape(1, T) * tlog[...].astype(F32)
    top = jnp.exp(scores - jnp.max(scores, axis=0, keepdims=True))
    teach[...] = top / jnp.sum(top, axis=0, keepdims=True)

    @pl.loop(0, VOC // 64)
    def _(part):
        first = pl.multiple_of(part * 64, 64)
        row = lax.broadcasted_iota(jnp.int32, (64, T), 0) + first
        found = jnp.zeros((64, T), F32)
        for k in range(TOP):
            found = jnp.where(row == rel_ids[k : k + 1, :], teach[k : k + 1, :], found)
        tgt[pl.ds(first, 64), :] = found

    def over(off):
        slot = z_at(off) * 2 + ox
        a_copy(c, slot, 0, x_peer).wait_recv()
        a_start(slot, core_peer)

    over(0)
    for off in NEAR:
        slot = z_at(off) * 2 + xl
        a_copy(c, slot, 0, z_peer(off)).wait_recv()
        a_start(slot, x_peer)
        a_start(slot, core_peer)
    for off in NEAR:
        over(off)
    logits = jnp.dot(wt[c], conv[c].reshape(ZX * CH, T), preferred_element_type=F32)

    @pl.loop(0, ZX)
    def _(slot):
        a_copy(oc, slot, 0, core_peer).wait_recv()

    logits = logits + jnp.dot(wt[oc], conv[oc].reshape(ZX * CH, T), preferred_element_type=F32)

    peak = jnp.max(logits, axis=0, keepdims=True)
    raised = jnp.exp(logits - peak)
    ex[...] = raised
    own = peak + jnp.log(jnp.sum(raised, axis=0, keepdims=True))
    stats[m] = own

    def b_copy(off, slot):
        return remote(
            stats.at[slot], stats.at[slot], b_send.at[off], b_recv.at[slot], {"mp": (m + off) % 32}
        )

    @pl.loop(1, 32)
    def _(off):
        b_copy(off, m).start()

    for copy in sent:
        copy.wait_send()

    @pl.loop(1, 32)
    def _(off):
        b_copy(off, (m + off) % 32).wait_recv()

    every = stats[...]
    most = jnp.max(every, axis=0)
    norm = most + jnp.log(jnp.sum(jnp.exp(every - most[None]), axis=0))
    factor = jnp.exp(peak - norm)
    live = lax.broadcasted_iota(jnp.int32, (1, T), 1) < used[0]
    gt[...] = jnp.where(live, ex[...] * factor - tgt[...], 0.0).astype(BF)

    core_copies = []
    for k, (side, core) in enumerate(((ox, oc), (xl, oc), (ox, c), (xl, c))):
        rows = w[:, side, core].reshape(NZ * CH, VOC)
        cg[k] = jnp.dot(rows, gt[...], preferred_element_type=F32).astype(BF).reshape(NZ, CH, T)
        if k < 2:
            copy = remote(cg.at[k], cin.at[k], dc_send.at[k], dc_recv.at[k], core_peer)
            copy.start()
            core_copies.append(copy)

    for half in range(2):
        for col in range(2):
            hh[half, col] = (
                lax.dot_general(
                    conv[half].reshape(ZX * CH, T),
                    gt[col * T : (col + 1) * T, :],
                    (((1,), (1,)), ((), ())),
                    preferred_element_type=F32,
                )
                .astype(BF)
                .reshape(ZX, CH, T)
            )

    def row_of(side, owner):
        return (oh if side == 0 else xh) * NY + owner

    def r_copy(way, dist, half, side, col, owner):
        at = (way, dist - 1, half, side, col)
        return remote(
            hh.at[half, col, row_of(side, owner)], rin.at[at], r_send.at[at], r_recv.at[at], y_peer(1 if way else -1)
        )

    def r_step(dist, late):
        for side in range(2):
            for col in range(2):
                for way in range(2):
                    owner = y_at(dist if way else -dist)
                    if dist == 4:
                        r_copy(way, dist, way, side, col, owner).start()
                        continue
                    half = way if late else 1 - way
                    if dist < 3 or late:
                        row = row_of(side, owner)
                        r_copy(way, dist + 1, half, side, col, owner).wait_recv()
                        hh[half, col, row] = (
                            hh[half, col, row].astype(F32) + rin[way, dist, half, side, col].astype(F32)
                        ).astype(BF)
                    r_copy(way, dist, half, side, col, owner).start()

    r_step(4, True)

    def dx_copy(slot):
        return remote(xsend.at[slot], xin.at[slot], dx_send.at[slot], dx_recv.at[slot], x_peer)

    core_copies[0].wait_recv()
    for off in (*FAR, 0):
        at = z_at(off)
        xsend[at] = (cg[2, at].astype(F32) + cin[0, at].astype(F32)).astype(BF)
        dx_copy(at).start()
    core_copies[1].wait_recv()

    def dz_copy(off, slot):
        return remote(zsend.at[slot], zin.at[off], dz_send.at[off], dz_recv.at[off], z_peer(off))

    def d_step(off):
        at = z_at(off)
        dx_copy(at).wait_recv()
        total = cg[3, at].astype(F32) + cin[1, at].astype(F32) + xin[at].astype(F32)
        if off == 0:
            grad[...] = total
            return
        zsend[at] = total.astype(BF)
        dz_copy(off, at).start()

    for side in range(2):
        for col in range(2):
            for way in range(2):
                r_copy(way, 4, way, side, col, y).wait_send()
    r_step(3, False)

    @pl.loop(1, 32)
    def _(off):
        b_copy(off, m).wait_send()

    for copy in core_copies:
        copy.wait_send()
    r_step(3, True)
    for off in (*FAR, 0):
        d_step(off)
    for off in (*FAR, 0):
        dx_copy(z_at(off)).wait_send()
    r_step(2, False)
    r_step(2, True)
    r_step(1, False)
    r_step(1, True)
    conv_grad = grad[...]
    for off in FAR:
        dz_copy(off, z_at(off)).wait_recv()
        conv_grad = conv_grad + zin[off].astype(F32)
    grad[...] = conv_grad

    group = lax.broadcasted_iota(jnp.int32, (1, 8, 128), 2)

    def k_terms(some, packed):
        for j in some:
            terms = xm[j] * grad[...]
            sums = jnp.sum(terms[:, :128] + terms[:, 128:], axis=1, keepdims=True).reshape(CH // 8, 8, 1)
            for g in range(3):
                packed = jnp.where(group == g * TAPS + j, sums[2 * g : 2 * g + 2], packed)
        return packed

    packed = k_terms(range(TAPS), jnp.zeros((2, 8, 128), F32))
    ky[d] = packed.reshape(16, 128)

    def k_copy(off, slot):
        return remote(ky.at[slot], ky.at[slot], k_send.at[off], k_recv.at[slot], {"dp": (d + off) % 16})

    @pl.loop(1, 16)
    def _(off):
        k_copy(off, d).start()

    def cx_copy(half, col):
        return remote(xfin.at[half, col], xrin.at[half, col], cx_send.at[half, col], cx_recv.at[half, col], h_peer)

    def y_total(half, col, side):
        total = hh[half, col, row_of(side, y)].astype(F32)
        for way in range(2):
            r_copy(way, 1, half, side, col, y).wait_recv()
            total = total + rin[way, 0, half, side, col].astype(F32)
        return total

    for half in range(2):
        for col in range(2):
            xfin[half, col] = y_total(half, col, 0).astype(BF)
            cx_copy(half, col).start()

    acc = jnp.zeros((CH, T), F32)
    for j in range(TAPS):
        delta = j - LEFT
        acc = acc + only(kept(-delta), moved(grad[...], -delta) * tap_t[:, j : j + 1])
    out_in[...] = acc

    for half in range(2):
        for col in range(2):
            out_h[half, :, col * T : (col + 1) * T] = y_total(half, col, 1)

    for off in FAR:
        dz_copy(off, z_at(off)).wait_send()
    for way in range(2):
        for side in range(2):
            for col in range(2):
                for dist in range(1, 4):
                    for half in range(2):
                        r_copy(way, dist, half, side, col, y).wait_send()

    @pl.loop(1, 16)
    def _(off):
        k_copy(off, d).wait_send()

    @pl.loop(1, 16)
    def _(off):
        k_copy(off, (d + off) % 16).wait_recv()

    flat = jnp.sum(ky[...], axis=0).T
    out_k[...] = jnp.concatenate([flat[g * TAPS : (g + 1) * TAPS, :] for g in range(3)], axis=1)

    for half in range(2):
        for col in range(2):
            cx_copy(half, col).wait_recv()
            cols = slice(col * T, (col + 1) * T)
            out_h[half, :, cols] = out_h[half, :, cols] + xrin[half, col].astype(F32)

    for half in range(2):
        for col in range(2):
            cx_copy(half, col).wait_send()


def put_out(a, b, c, out_a, out_b, out_c, sem):
    copies = [
        pltpu.make_async_copy(src, dst, sem.at[k]) for k, (src, dst) in enumerate(((c, out_c), (a, out_a), (b, out_b)))
    ]
    for copy in copies:
        copy.start()
    for copy in copies:
        copy.wait()


def local(frames, conv_kernel, head_weight, utterance_ids, tile_used, teacher_ids, teacher_logits, teacher_scale):
    vmem = pl.BlockSpec(memory_space=pltpu.VMEM)
    anywhere = pl.BlockSpec(memory_space=pl.ANY)
    dma = pltpu.SemaphoreType.DMA
    shapes = (
        jax.ShapeDtypeStruct((CH, T), F32),
        jax.ShapeDtypeStruct((TAPS, CH), F32),
        jax.ShapeDtypeStruct((2, CH, VOC), F32),
    )
    given = (
        frames.T,
        conv_kernel,
        head_weight.reshape(NZ, 2, 2, CH, VOC),
        utterance_ids,
        teacher_ids.T,
        teacher_logits.T,
        teacher_scale,
    )
    results = pl.pallas_call(
        kernel,
        out_shape=shapes,
        in_specs=[pl.BlockSpec(memory_space=pltpu.SMEM)] + [anywhere] * 7,
        out_specs=(vmem, vmem, vmem),
        scratch_shapes=[
            pltpu.VMEM((CH, T), BF),
            pltpu.VMEM((TAPS, CH), BF),
            pltpu.VMEM((1, T), jnp.int32),
            pltpu.VMEM((TOP, T), jnp.int32),
            pltpu.VMEM((TOP, T), jnp.int32),
            pltpu.VMEM((T,), F32),
            pltpu.VMEM((NZ, 2, 2, CH, VOC), BF),
            pltpu.VMEM((2, VOC, ZX * CH), BF),
            pltpu.VMEM((2, ZX, CH, T), BF),
            pltpu.VMEM((CH, T), F32),
            pltpu.VMEM((TAPS, CH, T), F32),
            pltpu.VMEM((8, T), jnp.int32),
            pltpu.VMEM((8, T), jnp.int32),
            pltpu.VMEM((TOP, T), jnp.int32),
            pltpu.VMEM((TOP, T), F32),
            pltpu.VMEM((VOC, T), F32),
            pltpu.VMEM((VOC, T), F32),
            pltpu.VMEM((32, 1, T), F32),
            pltpu.VMEM((VOC, T), BF),
            pltpu.VMEM((4, NZ, CH, T), BF),
            pltpu.VMEM((2, NZ, CH, T), BF),
            pltpu.VMEM((NZ, CH, T), BF),
            pltpu.VMEM((NZ, CH, T), BF),
            pltpu.VMEM((NZ, CH, T), BF),
            pltpu.VMEM((NZ, CH, T), BF),
            pltpu.VMEM((CH, T), F32),
            pltpu.VMEM((2, 2, ZX, CH, T), BF),
            pltpu.VMEM((2, 4, 2, 2, 2, CH, T), BF),
            pltpu.VMEM((2, 2, CH, T), BF),
            pltpu.VMEM((2, 2, CH, T), BF),
            pltpu.VMEM((16, 16, 128), F32),
            dma((7,)),
            dma((31,)),
            dma((2, ZX)),
            dma((32,)),
            dma((32,)),
            dma((2,)),
            dma((2,)),
            dma((NZ,)),
            dma((NZ,)),
            dma((NZ,)),
            dma((NZ,)),
            dma((2, 4, 2, 2, 2)),
            dma((2, 4, 2, 2, 2)),
            dma((2, 2)),
            dma((2, 2)),
            dma((16,)),
            dma((16,)),
        ],
        compiler_params=pltpu.CompilerParams(
            collective_id=0, has_side_effects=True, vmem_limit_bytes=24 * 1024 * 1024
        ),
    )(
        tile_used, *(pltpu.with_memory_space_constraint(value, pltpu.HBM) for value in given)
    )
    grad, kernel_grad, head = pl.pallas_call(
        put_out,
        out_shape=shapes,
        in_specs=[vmem] * 3,
        out_specs=(anywhere,) * 3,
        scratch_shapes=[dma((3,))],
        compiler_params=pltpu.CompilerParams(vmem_limit_bytes=4 * 1024 * 1024),
    )(*results)
    return grad.T, kernel_grad, head.reshape(2 * CH, VOC)


def solution(mesh):
    return jax.shard_map(
        local,
        mesh=mesh,
        in_specs=(
            P("dp", "mp"),
            P(None, "mp"),
            P(None, "mp"),
            P("dp", None),
            P("dp"),
            P("dp", None),
            P("dp", None),
            P("dp"),
        ),
        out_specs=(P("dp", "mp"), P(None, "mp"), P("dp", "mp")),
        check_vma=False,
    )
```

```python
import jax
import jax.numpy as jnp
from jax import lax
from jax.experimental import pallas as pl
from jax.experimental.pallas import tpu as pltpu
from jax.sharding import PartitionSpec as P

MESH = pl.DeviceIdType.MESH
TAPS = 32
LEFT = (TAPS - 1) // 2
TOP = 32
NZ = 8
NY = 8
CH = 48
T = 256
VOC = 512
ZX = 16
F32 = jnp.float32
BF = jnp.bfloat16

NEAR = (1, 7, 2, 6, 3, 5, 4)
FAR = (4, 3, 5, 2, 6, 1, 7)
SENDS = (4, 1, 7, 2, 6, 3, 5)


def eye(n):
    same = lax.broadcasted_iota(jnp.int32, (n, n), 0) == lax.broadcasted_iota(jnp.int32, (n, n), 1)
    return jnp.where(same, 1.0, 0.0).astype(BF)


def turned(values):
    return lax.dot_general(
        eye(values.shape[1]), values, (((1,), (1,)), ((), ())), preferred_element_type=F32
    )


def kernel(
    used, frames_hbm, taps_hbm, w_hbm, seg_hbm, ids_hbm, tlog_hbm, scale_hbm,
    out_in, out_k, out_h,
    frames, taps, seg, ids, tlog, scale,
    w, wt, conv, xt, xm, src_rows, dst_rows, rel_ids, teach, tgt, ex, stats, gt,
    cg, cin, zsend, zin, grad,
    h4, hh, rin, xrin, ky,
    in_sem, a_send, a_recv, b_send, b_recv, dc_send, dc_recv, dz_send, dz_recv,
    r_send, r_recv, cx_send, cx_recv, k_send, k_recv, column_sem,
):
    m = lax.axis_index("mp")
    d = lax.axis_index("dp")
    c, xl, z = m % 2, (m // 2) % 2, m // 4
    y, xh = d % NY, d // NY
    zx = m // 2
    oc, ox, oh = 1 - c, 1 - xl, 1 - xh
    core_peer = {"mp": m + 1 - 2 * c}
    x_peer = {"mp": m + 2 - 4 * xl}
    h_peer = {"dp": oh * NY + y}

    def z_at(off):
        return (z + off) % NZ

    def z_peer(off):
        return {"mp": z_at(off) * 4 + xl * 2 + c}

    def y_at(off):
        return (y + off + NY) % NY

    def y_peer(off):
        return {"dp": xh * NY + y_at(off)}

    pairs = (
        (frames_hbm, frames), (taps_hbm, taps), (seg_hbm, seg),
        (w_hbm, w), (ids_hbm, ids), (tlog_hbm, tlog), (scale_hbm, scale),
    )
    loads = [pltpu.make_async_copy(src, dst, in_sem.at[k]) for k, (src, dst) in enumerate(pairs)]
    for load in loads:
        load.start()

    barrier = pltpu.get_barrier_semaphore()

    near = [z_peer(off) for off in FAR] + [y_peer(off) for off in FAR] + [x_peer, core_peer, h_peer]
    for peer in near:
        pl.semaphore_signal(barrier, inc=1, device_id=peer, device_id_type=MESH)

    def remote(src, dst, send, recv, peer):
        return pltpu.make_async_remote_copy(
            src_ref=src, dst_ref=dst, send_sem=send, recv_sem=recv, device_id=peer, device_id_type=MESH
        )

    for load in loads[:3]:
        load.wait()

    lane = lax.broadcasted_iota(jnp.int32, (8, T), 1)
    valid = lane < used[0]
    seg_rows = jnp.broadcast_to(seg[...], (8, T))
    src_rows[...] = jnp.where(valid, seg_rows, -1)
    dst_rows[...] = jnp.where(valid, seg_rows, -2)
    xt[...] = frames[...].astype(F32)
    tap_t = turned(taps[...])

    def kept(delta):
        rolled = src_rows[...]
        if delta:
            rolled = pltpu.roll(rolled, (-delta) % T, 1)
        keep = rolled == dst_rows[...]
        if delta > 0:
            keep = keep & (lane < T - delta)
        if delta < 0:
            keep = keep & (lane >= -delta)
        return keep

    def moved(values, delta):
        return pltpu.roll(values, (-delta) % T, 1) if delta else values

    def only(keep, values):
        return jnp.where(keep[None], values.reshape(CH // 8, 8, T), 0.0).reshape(CH, T)

    acc = jnp.zeros((CH, T), F32)
    for j in range(TAPS):
        delta = j - LEFT
        source = only(kept(delta), moved(xt[...], delta))
        xm[j] = source
        acc = acc + source * tap_t[:, j : j + 1]
    conv[c, zx] = acc.astype(BF)

    pl.semaphore_wait(barrier, len(near))
    pl.semaphore_signal(column_sem, inc=1, device_id=h_peer, device_id_type=MESH)

    def a_copy(slot_c, slot_zx, k, peer):
        return remote(
            conv.at[slot_c, slot_zx], conv.at[slot_c, slot_zx], a_send.at[k], a_recv.at[slot_c, slot_zx], peer
        )

    sent = []

    def a_start(slot, peer):
        copy = a_copy(c, slot, len(sent), peer)
        copy.start()
        sent.append(copy)

    a_start(zx, x_peer)
    a_start(zx, core_peer)
    for off in SENDS:
        a_start(zx, z_peer(off))

    for load in loads[3:]:
        load.wait()
    for half in range(2):
        for v in range(VOC // 128):
            part = w[:, :, half, :, v * 128 : (v + 1) * 128].reshape(ZX * CH, 128)
            wt[half, v * 128 : (v + 1) * 128, :] = part.T

    rel_ids[...] = ids[...] - m * VOC
    scores = scale[...].reshape(1, T) * tlog[...].astype(F32)
    top = jnp.exp(scores - jnp.max(scores, axis=0, keepdims=True))
    teach[...] = top / jnp.sum(top, axis=0, keepdims=True)

    @pl.loop(0, VOC // 64)
    def _(part):
        first = pl.multiple_of(part * 64, 64)
        row = lax.broadcasted_iota(jnp.int32, (64, T), 0) + first
        found = jnp.zeros((64, T), F32)
        for k in range(TOP):
            found = jnp.where(row == rel_ids[k : k + 1, :], teach[k : k + 1, :], found)
        tgt[pl.ds(first, 64), :] = found

    def over(off):
        slot = z_at(off) * 2 + ox
        a_copy(c, slot, 0, x_peer).wait_recv()
        a_start(slot, core_peer)

    over(0)
    for off in NEAR:
        slot = z_at(off) * 2 + xl
        a_copy(c, slot, 0, z_peer(off)).wait_recv()
        a_start(slot, x_peer)
        a_start(slot, core_peer)
    for off in NEAR:
        over(off)
    logits = jnp.dot(wt[c], conv[c].reshape(ZX * CH, T), preferred_element_type=F32)

    @pl.loop(0, ZX)
    def _(slot):
        a_copy(oc, slot, 0, core_peer).wait_recv()

    logits = logits + jnp.dot(wt[oc], conv[oc].reshape(ZX * CH, T), preferred_element_type=F32)

    peak = jnp.max(logits, axis=0, keepdims=True)
    raised = jnp.exp(logits - peak)
    ex[...] = raised
    own = peak + jnp.log(jnp.sum(raised, axis=0, keepdims=True))
    stats[m] = own

    def b_copy(off, slot):
        return remote(
            stats.at[slot], stats.at[slot], b_send.at[off], b_recv.at[slot], {"mp": (m + off) % 32}
        )

    @pl.loop(1, 32)
    def _(off):
        b_copy(off, m).start()

    for copy in sent:
        copy.wait_send()

    @pl.loop(1, 32)
    def _(off):
        b_copy(off, (m + off) % 32).wait_recv()

    every = stats[...]
    most = jnp.max(every, axis=0)
    norm = most + jnp.log(jnp.sum(jnp.exp(every - most[None]), axis=0))
    factor = jnp.exp(peak - norm)
    live = lax.broadcasted_iota(jnp.int32, (1, T), 1) < used[0]
    gt[...] = jnp.where(live, ex[...] * factor - tgt[...], 0.0).astype(BF)

    def row_of(side, owner):
        return (oh if side == 0 else xh) * NY + owner

    def r_copy(way, dist, half, side, col, owner):
        at = (way, dist - 1, half, side, col)
        peer = y_peer(1 if way else -1)
        if dist == 1 and side == 0:
            peer = {"dp": oh * NY + y_at(1 if way else -1)}
        src = h4.at[half, side, col] if dist == 4 else hh.at[half, col, row_of(side, owner)]
        return remote(src, rin.at[at], r_send.at[at], r_recv.at[at], peer)

    def r_step(dist, late):
        for side in range(2):
            for col in range(2):
                for way in range(2):
                    owner = y_at(dist if way else -dist)
                    if dist == 4:
                        r_copy(way, dist, way, side, col, owner).start()
                        continue
                    half = way if late else 1 - way
                    if dist < 3 or late:
                        row = row_of(side, owner)
                        r_copy(way, dist + 1, half, side, col, owner).wait_recv()
                        hh[half, col, row] = (
                            hh[half, col, row].astype(F32) + rin[way, dist, half, side, col].astype(F32)
                        ).astype(BF)
                    r_copy(way, dist, half, side, col, owner).start()

    spots = [(half, side) for half in range(2) for side in range(2)]
    rows = jnp.concatenate([conv[half, row_of(side, y_at(4))] for half, side in spots])
    for col in range(2):
        part = lax.dot_general(
            rows, gt[col * T : (col + 1) * T, :], (((1,), (1,)), ((), ())), preferred_element_type=F32
        ).astype(BF)
        for k, (half, side) in enumerate(spots):
            h4[half, side, col] = part[k * CH : (k + 1) * CH]
    r_step(4, True)

    core_copies = []
    for core in (oc, c):
        rows = jnp.concatenate([w[:, side, core].reshape(NZ * CH, VOC) for side in (ox, xl)])
        terms = jnp.dot(rows, gt[...], preferred_element_type=F32).astype(BF)
        for side in range(2):
            k = side if core is oc else side + 2
            cg[k] = terms[side * NZ * CH : (side + 1) * NZ * CH].reshape(NZ, CH, T)
            if k < 2:
                copy = remote(cg.at[k], cin.at[k], dc_send.at[k], dc_recv.at[k], core_peer)
                copy.start()
                core_copies.append(copy)

    def d_copy(i, off):
        peer = {"mp": z_at(off) * 4 + (xl if i else ox) * 2 + c}
        return remote(zsend.at[i, off], zin.at[i, off], dz_send.at[i, off], dz_recv.at[i, off], peer)

    d_moves = [(i, off) for i in range(2) for off in (*FAR, 0) if (i, off) != (1, 0)]
    core_copies[0].wait_recv()
    for i, off in d_moves:
        if (i, off) == (1, FAR[0]):
            core_copies[1].wait_recv()
        at = z_at(off)
        zsend[i, off] = (cg[2 + i, at].astype(F32) + cin[i, at].astype(F32)).astype(BF)
        d_copy(i, off).start()
    grad[...] = cg[3, z].astype(F32) + cin[1, z].astype(F32)

    for half in range(2):
        for col in range(2):
            hh[half, col] = (
                lax.dot_general(
                    conv[half].reshape(ZX * CH, T),
                    gt[col * T : (col + 1) * T, :],
                    (((1,), (1,)), ((), ())),
                    preferred_element_type=F32,
                )
                .astype(BF)
                .reshape(ZX, CH, T)
            )

    r_step(3, False)
    for side in range(2):
        for col in range(2):
            for way in range(2):
                r_copy(way, 4, way, side, col, y).wait_send()

    @pl.loop(1, 32)
    def _(off):
        b_copy(off, m).wait_send()

    for copy in core_copies:
        copy.wait_send()
    r_step(3, True)
    r_step(2, False)
    r_step(2, True)

    def cx_copy(half, col):
        return remote(
            hh.at[half, col, row_of(0, y)],
            xrin.at[half, col],
            cx_send.at[half, col],
            cx_recv.at[half, col],
            h_peer,
        )

    for half in range(2):
        for col in range(2):
            cx_copy(half, col).start()
    pl.semaphore_wait(column_sem, 1)
    r_step(1, False)
    conv_grad = grad[...]
    for i, off in d_moves:
        d_copy(i, off).wait_recv()
        conv_grad = conv_grad + zin[i, off].astype(F32)
    grad[...] = conv_grad

    group = lax.broadcasted_iota(jnp.int32, (1, 8, 128), 2)
    packed = jnp.zeros((2, 8, 128), F32)
    for j in range(TAPS):
        terms = xm[j] * grad[...]
        sums = jnp.sum(terms[:, :128] + terms[:, 128:], axis=1, keepdims=True).reshape(CH // 8, 8, 1)
        for g in range(3):
            packed = jnp.where(group == g * TAPS + j, sums[2 * g : 2 * g + 2], packed)
    ky[d] = packed.reshape(16, 128).astype(BF)

    def k_copy(off, slot):
        return remote(ky.at[slot], ky.at[slot], k_send.at[off], k_recv.at[slot], {"dp": (d + off) % 16})

    @pl.loop(1, 16)
    def _(off):
        k_copy(off, d).start()

    r_step(1, True)

    acc = jnp.zeros((CH, T), F32)
    for j in range(TAPS):
        delta = j - LEFT
        acc = acc + only(kept(-delta), moved(grad[...], -delta) * tap_t[:, j : j + 1])
    out_in[...] = acc

    for i, off in d_moves:
        d_copy(i, off).wait_send()
    for way in range(2):
        for side in range(2):
            for col in range(2):
                for dist in range(2, 4):
                    for half in range(2):
                        r_copy(way, dist, half, side, col, y).wait_send()
    for half in range(2):
        for col in range(2):
            cx_copy(half, col).wait_send()

    def y_total(half, col, total, sides):
        for side in sides:
            for way in range(2):
                r_copy(way, 1, half, side, col, y).wait_recv()
                total = total + rin[way, 0, half, side, col].astype(F32)
        return total

    for half in range(2):
        for col in range(2):
            cx_copy(half, col).wait_recv()

    for half in range(2):
        for col in range(2):
            total = hh[half, col, row_of(1, y)].astype(F32) + xrin[half, col].astype(F32)
            out_h[half, :, col * T : (col + 1) * T] = y_total(half, col, total, (1,))

    @pl.loop(1, 16)
    def _(off):
        k_copy(off, (d + off) % 16).wait_recv()

    flat = jnp.sum(ky[...].astype(F32), axis=0).T
    out_k[...] = jnp.concatenate([flat[g * TAPS : (g + 1) * TAPS, :] for g in range(3)], axis=1)

    for half in range(2):
        for col in range(2):
            cols = slice(col * T, (col + 1) * T)
            out_h[half, :, cols] = y_total(half, col, out_h[half, :, cols], (0,))

    for way in range(2):
        for side in range(2):
            for col in range(2):
                for half in range(2):
                    r_copy(way, 1, half, side, col, y).wait_send()

    @pl.loop(1, 16)
    def _(off):
        k_copy(off, d).wait_send()


def put_out(a, b, c, out_a, out_b, out_c, sem):
    copies = [
        pltpu.make_async_copy(src, dst, sem.at[k]) for k, (src, dst) in enumerate(((c, out_c), (a, out_a), (b, out_b)))
    ]
    for copy in copies:
        copy.start()
    for copy in copies:
        copy.wait()


def local(frames, conv_kernel, head_weight, utterance_ids, tile_used, teacher_ids, teacher_logits, teacher_scale):
    vmem = pl.BlockSpec(memory_space=pltpu.VMEM)
    anywhere = pl.BlockSpec(memory_space=pl.ANY)
    dma = pltpu.SemaphoreType.DMA
    shapes = (
        jax.ShapeDtypeStruct((CH, T), F32),
        jax.ShapeDtypeStruct((TAPS, CH), F32),
        jax.ShapeDtypeStruct((2, CH, VOC), F32),
    )
    given = (
        frames.T,
        conv_kernel,
        head_weight.reshape(NZ, 2, 2, CH, VOC),
        utterance_ids,
        teacher_ids.T,
        teacher_logits.T,
        teacher_scale,
    )
    results = pl.pallas_call(
        kernel,
        out_shape=shapes,
        in_specs=[pl.BlockSpec(memory_space=pltpu.SMEM)] + [anywhere] * 7,
        out_specs=(vmem, vmem, vmem),
        scratch_shapes=[
            pltpu.VMEM((CH, T), BF),
            pltpu.VMEM((TAPS, CH), BF),
            pltpu.VMEM((1, T), jnp.int32),
            pltpu.VMEM((TOP, T), jnp.int32),
            pltpu.VMEM((TOP, T), jnp.int32),
            pltpu.VMEM((T,), F32),
            pltpu.VMEM((NZ, 2, 2, CH, VOC), BF),
            pltpu.VMEM((2, VOC, ZX * CH), BF),
            pltpu.VMEM((2, ZX, CH, T), BF),
            pltpu.VMEM((CH, T), F32),
            pltpu.VMEM((TAPS, CH, T), F32),
            pltpu.VMEM((8, T), jnp.int32),
            pltpu.VMEM((8, T), jnp.int32),
            pltpu.VMEM((TOP, T), jnp.int32),
            pltpu.VMEM((TOP, T), F32),
            pltpu.VMEM((VOC, T), F32),
            pltpu.VMEM((VOC, T), F32),
            pltpu.VMEM((32, 1, T), F32),
            pltpu.VMEM((VOC, T), BF),
            pltpu.VMEM((4, NZ, CH, T), BF),
            pltpu.VMEM((2, NZ, CH, T), BF),
            pltpu.VMEM((2, NZ, CH, T), BF),
            pltpu.VMEM((2, NZ, CH, T), BF),
            pltpu.VMEM((CH, T), F32),
            pltpu.VMEM((2, 2, 2, CH, T), BF),
            pltpu.VMEM((2, 2, ZX, CH, T), BF),
            pltpu.VMEM((2, 4, 2, 2, 2, CH, T), BF),
            pltpu.VMEM((2, 2, CH, T), BF),
            pltpu.VMEM((16, 16, 128), BF),
            dma((7,)),
            dma((31,)),
            dma((2, ZX)),
            dma((32,)),
            dma((32,)),
            dma((2,)),
            dma((2,)),
            dma((2, NZ)),
            dma((2, NZ)),
            dma((2, 4, 2, 2, 2)),
            dma((2, 4, 2, 2, 2)),
            dma((2, 2)),
            dma((2, 2)),
            dma((16,)),
            dma((16,)),
            pltpu.SemaphoreType.REGULAR,
        ],
        compiler_params=pltpu.CompilerParams(
            collective_id=0, has_side_effects=True, vmem_limit_bytes=24 * 1024 * 1024
        ),
    )(
        tile_used, *(pltpu.with_memory_space_constraint(value, pltpu.HBM) for value in given)
    )
    grad, kernel_grad, head = pl.pallas_call(
        put_out,
        out_shape=shapes,
        in_specs=[vmem] * 3,
        out_specs=(anywhere,) * 3,
        scratch_shapes=[dma((3,))],
        compiler_params=pltpu.CompilerParams(vmem_limit_bytes=4 * 1024 * 1024),
    )(*results)
    return grad.T, kernel_grad, head.reshape(2 * CH, VOC)


def solution(mesh):
    return jax.shard_map(
        local,
        mesh=mesh,
        in_specs=(
            P("dp", "mp"),
            P(None, "mp"),
            P(None, "mp"),
            P("dp", None),
            P("dp"),
            P("dp", None),
            P("dp", None),
            P("dp"),
        ),
        out_specs=(P("dp", "mp"), P(None, "mp"), P("dp", "mp")),
        check_vma=False,
    )
```

```python
import jax
import jax.numpy as jnp
from jax import lax
from jax.experimental import pallas as pl
from jax.experimental.pallas import tpu as pltpu
from jax.sharding import PartitionSpec as P

MESH = pl.DeviceIdType.MESH
TAPS = 32
LEFT = (TAPS - 1) // 2
TOP = 32
NZ = 8
NY = 8
CH = 48
T = 256
VOC = 512
ZX = 16
F32 = jnp.float32
BF = jnp.bfloat16

NEAR = (1, 7, 2, 6, 3, 5, 4)
FAR = (4, 3, 5, 2, 6, 1, 7)
SENDS = (4, 1, 7, 2, 6, 3, 5)


def eye(n):
    same = lax.broadcasted_iota(jnp.int32, (n, n), 0) == lax.broadcasted_iota(jnp.int32, (n, n), 1)
    return jnp.where(same, 1.0, 0.0).astype(BF)


def turned(values):
    return lax.dot_general(
        eye(values.shape[1]), values, (((1,), (1,)), ((), ())), preferred_element_type=F32
    )


def kernel(
    used, frames_hbm, taps_hbm, w_hbm, seg_hbm, ids_hbm, tlog_hbm, scale_hbm,
    out_in, out_k, out_h,
    frames, taps, seg, ids, tlog, scale,
    w, wt, conv, xt, xm, src_rows, dst_rows, rel_ids, teach, tgt, ex, stats, gt,
    cg, cin, zsend, zin, grad,
    h4, hh, rin, xrin, ky,
    in_sem, a_send, a_recv, a_core, b_send, b_recv, dc_send, dc_recv, dz_send, dz_recv,
    r_send, r_recv, r4_recv, r1_recv, cx_send, cx_recv, k_send, k_recv, column_sem,
):
    m = lax.axis_index("mp")
    d = lax.axis_index("dp")
    c, xl, z = m % 2, (m // 2) % 2, m // 4
    y, xh = d % NY, d // NY
    zx = m // 2
    oc, ox, oh = 1 - c, 1 - xl, 1 - xh
    core_peer = {"mp": m + 1 - 2 * c}
    x_peer = {"mp": m + 2 - 4 * xl}
    h_peer = {"dp": oh * NY + y}

    def z_at(off):
        return (z + off) % NZ

    def z_peer(off):
        return {"mp": z_at(off) * 4 + xl * 2 + c}

    def y_at(off):
        return (y + off + NY) % NY

    def y_peer(off):
        return {"dp": xh * NY + y_at(off)}

    pairs = (
        (frames_hbm, frames), (taps_hbm, taps), (seg_hbm, seg),
        (w_hbm, w), (ids_hbm, ids), (tlog_hbm, tlog), (scale_hbm, scale),
    )
    loads = [pltpu.make_async_copy(src, dst, in_sem.at[k]) for k, (src, dst) in enumerate(pairs)]
    for load in loads:
        load.start()

    barrier = pltpu.get_barrier_semaphore()

    near = [z_peer(off) for off in FAR] + [y_peer(off) for off in FAR] + [x_peer, core_peer, h_peer]
    for peer in near:
        pl.semaphore_signal(barrier, inc=1, device_id=peer, device_id_type=MESH)

    def remote(src, dst, send, recv, peer):
        return pltpu.make_async_remote_copy(
            src_ref=src, dst_ref=dst, send_sem=send, recv_sem=recv, device_id=peer, device_id_type=MESH
        )

    for load in loads[:3]:
        load.wait()

    lane = lax.broadcasted_iota(jnp.int32, (8, T), 1)
    valid = lane < used[0]
    seg_rows = jnp.broadcast_to(seg[...], (8, T))
    src_rows[...] = jnp.where(valid, seg_rows, -1)
    dst_rows[...] = jnp.where(valid, seg_rows, -2)
    xt[...] = frames[...].astype(F32)
    tap_t = turned(taps[...])

    def kept(delta):
        rolled = src_rows[...]
        if delta:
            rolled = pltpu.roll(rolled, (-delta) % T, 1)
        keep = rolled == dst_rows[...]
        if delta > 0:
            keep = keep & (lane < T - delta)
        if delta < 0:
            keep = keep & (lane >= -delta)
        return keep

    def moved(values, delta):
        return pltpu.roll(values, (-delta) % T, 1) if delta else values

    def only(keep, values):
        return jnp.where(keep[None], values.reshape(CH // 8, 8, T), 0.0).reshape(CH, T)

    acc = jnp.zeros((CH, T), F32)
    for j in range(TAPS):
        delta = j - LEFT
        source = only(kept(delta), moved(xt[...], delta))
        xm[j] = source
        acc = acc + source * tap_t[:, j : j + 1]
    conv[c * ZX + zx] = acc.astype(BF)

    pl.semaphore_wait(barrier, len(near))
    pl.semaphore_signal(column_sem, inc=1, device_id=h_peer, device_id_type=MESH)

    def a_copy(slot, peer):
        block = conv.at[c * ZX + slot]
        return remote(block, block, a_send, a_core if peer is core_peer else a_recv.at[slot], peer)

    def a_start(slot, peer):
        a_copy(slot, peer).start()

    a_start(zx, x_peer)
    a_start(zx, core_peer)
    for off in SENDS:
        a_start(zx, z_peer(off))

    for load in loads[3:]:
        load.wait()
    for half in range(2):
        for v in range(VOC // 128):
            part = w[:, :, half, :, v * 128 : (v + 1) * 128].reshape(ZX * CH, 128)
            wt[half, v * 128 : (v + 1) * 128, :] = part.T

    rel_ids[...] = ids[...] - m * VOC
    scores = scale[...].reshape(1, T) * tlog[...].astype(F32)
    top = jnp.exp(scores - jnp.max(scores, axis=0, keepdims=True))
    teach[...] = top / jnp.sum(top, axis=0, keepdims=True)

    @pl.loop(0, VOC // 64)
    def _(part):
        first = pl.multiple_of(part * 64, 64)
        row = lax.broadcasted_iota(jnp.int32, (64, T), 0) + first
        found = jnp.zeros((64, T), F32)
        for k in range(TOP):
            found = jnp.where(row == rel_ids[k : k + 1, :], teach[k : k + 1, :], found)
        tgt[pl.ds(first, 64), :] = found

    def over(off):
        slot = z_at(off) * 2 + ox
        a_copy(slot, x_peer).wait_recv()
        a_start(slot, core_peer)

    over(0)
    for off in NEAR:
        slot = z_at(off) * 2 + xl
        a_copy(slot, z_peer(off)).wait_recv()
        a_start(slot, x_peer)
        a_start(slot, core_peer)
    for off in NEAR:
        over(off)
    def half_of(core):
        return conv[pl.ds(core * ZX, ZX)].reshape(ZX * CH, T)

    def several(ref, count, send, recv):
        some = ref.at[pl.ds(0, count)]
        return remote(some, some, send, recv, core_peer)

    logits = jnp.dot(wt[c], half_of(c), preferred_element_type=F32)
    several(conv, ZX, a_send, a_core).wait_recv()
    logits = logits + jnp.dot(wt[oc], half_of(oc), preferred_element_type=F32)

    peak = jnp.max(logits, axis=0, keepdims=True)
    raised = jnp.exp(logits - peak)
    ex[...] = raised
    own = peak + jnp.log(jnp.sum(raised, axis=0, keepdims=True))
    stats[m] = own

    def b_copy(off, slot):
        return remote(
            stats.at[slot], stats.at[slot], b_send, b_recv, {"mp": (m + off) % 32}
        )

    @pl.loop(1, 32)
    def _(off):
        b_copy(off, m).start()

    several(conv, 31, a_send, a_core).wait_send()
    several(stats, 31, b_send, b_recv).wait_recv()

    every = stats[...]
    most = jnp.max(every, axis=0)
    norm = most + jnp.log(jnp.sum(jnp.exp(every - most[None]), axis=0))
    factor = jnp.exp(peak - norm)
    live = lax.broadcasted_iota(jnp.int32, (1, T), 1) < used[0]
    gt[...] = jnp.where(live, ex[...] * factor - tgt[...], 0.0).astype(BF)

    def row_of(side, owner):
        return (oh if side == 0 else xh) * NY + owner

    def hh_at(half, col, side, owner):
        return (half * 2 + col) * ZX + row_of(side, owner)

    def r_copy(way, dist, half, side, col, owner):
        recv = r4_recv.at[way, side, col] if dist == 4 else r_recv.at[way, dist - 2, half, side, col]
        if dist == 1:
            recv = r1_recv.at[side]
        peer = y_peer(1 if way else -1)
        if dist == 1 and side == 0:
            peer = {"dp": oh * NY + y_at(1 if way else -1)}
        src = h4.at[half, side, col] if dist == 4 else hh.at[hh_at(half, col, side, owner)]
        return remote(src, rin.at[way, dist - 1, half, side, col], r_send, recv, peer)

    def r_step(dist, late):
        for side in range(2):
            for col in range(2):
                for way in range(2):
                    owner = y_at(dist if way else -dist)
                    if dist == 4:
                        r_copy(way, dist, way, side, col, owner).start()
                        continue
                    half = way if late else 1 - way
                    if dist < 3 or late:
                        row = hh_at(half, col, side, owner)
                        r_copy(way, dist + 1, half, side, col, owner).wait_recv()
                        hh[row] = (
                            hh[row].astype(F32) + rin[way, dist, half, side, col].astype(F32)
                        ).astype(BF)
                    r_copy(way, dist, half, side, col, owner).start()

    spots = [(half, side) for half in range(2) for side in range(2)]
    rows = jnp.concatenate([conv[half * ZX + row_of(side, y_at(4))] for half, side in spots])
    for col in range(2):
        part = lax.dot_general(
            rows, gt[col * T : (col + 1) * T, :], (((1,), (1,)), ((), ())), preferred_element_type=F32
        ).astype(BF)
        for k, (half, side) in enumerate(spots):
            h4[half, side, col] = part[k * CH : (k + 1) * CH]
    r_step(4, True)

    core_copies = []
    for core in (oc, c):
        rows = jnp.concatenate([w[:, side, core].reshape(NZ * CH, VOC) for side in (ox, xl)])
        terms = jnp.dot(rows, gt[...], preferred_element_type=F32).astype(BF)
        for side in range(2):
            k = side if core is oc else side + 2
            cg[k] = terms[side * NZ * CH : (side + 1) * NZ * CH].reshape(NZ, CH, T)
            if k < 2:
                copy = remote(cg.at[k], cin.at[k], dc_send, dc_recv.at[k], core_peer)
                copy.start()
                core_copies.append(copy)

    def d_copy(i, off):
        peer = {"mp": z_at(off) * 4 + (xl if i else ox) * 2 + c}
        return remote(zsend.at[i * NZ + off], zin.at[i * NZ + off], dz_send, dz_recv, peer)

    d_moves = [(i, off) for i in range(2) for off in (*FAR, 0) if (i, off) != (1, 0)]
    core_copies[0].wait_recv()
    for i, off in d_moves:
        if (i, off) == (1, FAR[0]):
            core_copies[1].wait_recv()
        at = z_at(off)
        zsend[i * NZ + off] = (cg[2 + i, at].astype(F32) + cin[i, at].astype(F32)).astype(BF)
        d_copy(i, off).start()
    grad[...] = cg[3, z].astype(F32) + cin[1, z].astype(F32)

    for half in range(2):
        for col in range(2):
            hh[(half * 2 + col) * ZX : (half * 2 + col + 1) * ZX] = (
                lax.dot_general(
                    half_of(half),
                    gt[col * T : (col + 1) * T, :],
                    (((1,), (1,)), ((), ())),
                    preferred_element_type=F32,
                )
                .astype(BF)
                .reshape(ZX, CH, T)
            )

    r_step(3, False)
    several(stats, 31, b_send, b_recv).wait_send()
    several(cg, 2, dc_send, dc_recv.at[0]).wait_send()
    r_step(3, True)
    r_step(2, False)
    r_step(2, True)

    def cx_copy(half, col):
        return remote(
            hh.at[hh_at(half, col, 0, y)],
            xrin.at[half, col],
            cx_send,
            cx_recv,
            h_peer,
        )

    for half in range(2):
        for col in range(2):
            cx_copy(half, col).start()
    pl.semaphore_wait(column_sem, 1)
    r_step(1, False)
    conv_grad = grad[...]
    several(zin, 15, dz_send, dz_recv).wait_recv()
    for i, off in d_moves:
        conv_grad = conv_grad + zin[i * NZ + off].astype(F32)
    grad[...] = conv_grad

    group = lax.broadcasted_iota(jnp.int32, (1, 8, 128), 2)
    packed = jnp.zeros((2, 8, 128), F32)
    for j in range(TAPS):
        terms = xm[j] * grad[...]
        sums = jnp.sum(terms[:, :128] + terms[:, 128:], axis=1, keepdims=True).reshape(CH // 8, 8, 1)
        for g in range(3):
            packed = jnp.where(group == g * TAPS + j, sums[2 * g : 2 * g + 2], packed)
    ky[d] = packed.reshape(16, 128).astype(BF)

    def k_copy(off, slot):
        return remote(ky.at[slot], ky.at[slot], k_send, k_recv, {"dp": (d + off) % 16})

    @pl.loop(1, 16)
    def _(off):
        k_copy(off, d).start()

    r_step(1, True)

    acc = jnp.zeros((CH, T), F32)
    for j in range(TAPS):
        delta = j - LEFT
        acc = acc + only(kept(-delta), moved(grad[...], -delta) * tap_t[:, j : j + 1])
    out_in[...] = acc

    several(zin, 15, dz_send, dz_recv).wait_send()
    several(hh, 4, cx_send, cx_recv).wait_send()

    several(hh, 4, cx_send, cx_recv).wait_recv()

    def y_total(half, col, total, side):
        for way in range(2):
            total = total + rin[way, 0, half, side, col].astype(F32)
        return total

    several(hh, 8, r_send, r1_recv.at[1]).wait_recv()
    for half in range(2):
        for col in range(2):
            total = hh[hh_at(half, col, 1, y)].astype(F32) + xrin[half, col].astype(F32)
            out_h[half, :, col * T : (col + 1) * T] = y_total(half, col, total, 1)

    several(ky, 15, k_send, k_recv).wait_recv()
    flat = jnp.sum(ky[...].astype(F32), axis=0).T
    out_k[...] = jnp.concatenate([flat[g * TAPS : (g + 1) * TAPS, :] for g in range(3)], axis=1)

    several(hh, 8, r_send, r1_recv.at[0]).wait_recv()
    for half in range(2):
        for col in range(2):
            cols = slice(col * T, (col + 1) * T)
            out_h[half, :, cols] = y_total(half, col, out_h[half, :, cols], 0)

    several(hh, 56, r_send, r1_recv.at[0]).wait_send()
    several(ky, 15, k_send, k_recv).wait_send()


def put_out(a, b, c, out_a, out_b, out_c, sem):
    copies = [
        pltpu.make_async_copy(src, dst, sem.at[k]) for k, (src, dst) in enumerate(((c, out_c), (a, out_a), (b, out_b)))
    ]
    for copy in copies:
        copy.start()
    for copy in copies:
        copy.wait()


def local(frames, conv_kernel, head_weight, utterance_ids, tile_used, teacher_ids, teacher_logits, teacher_scale):
    vmem = pl.BlockSpec(memory_space=pltpu.VMEM)
    anywhere = pl.BlockSpec(memory_space=pl.ANY)
    dma = pltpu.SemaphoreType.DMA
    shapes = (
        jax.ShapeDtypeStruct((CH, T), F32),
        jax.ShapeDtypeStruct((TAPS, CH), F32),
        jax.ShapeDtypeStruct((2, CH, VOC), F32),
    )
    given = (
        frames.T,
        conv_kernel,
        head_weight.reshape(NZ, 2, 2, CH, VOC),
        utterance_ids,
        teacher_ids.T,
        teacher_logits.T,
        teacher_scale,
    )
    results = pl.pallas_call(
        kernel,
        out_shape=shapes,
        in_specs=[pl.BlockSpec(memory_space=pltpu.SMEM)] + [anywhere] * 7,
        out_specs=(vmem, vmem, vmem),
        scratch_shapes=[
            pltpu.VMEM((CH, T), BF),
            pltpu.VMEM((TAPS, CH), BF),
            pltpu.VMEM((1, T), jnp.int32),
            pltpu.VMEM((TOP, T), jnp.int32),
            pltpu.VMEM((TOP, T), jnp.int32),
            pltpu.VMEM((T,), F32),
            pltpu.VMEM((NZ, 2, 2, CH, VOC), BF),
            pltpu.VMEM((2, VOC, ZX * CH), BF),
            pltpu.VMEM((2 * ZX, CH, T), BF),
            pltpu.VMEM((CH, T), F32),
            pltpu.VMEM((TAPS, CH, T), F32),
            pltpu.VMEM((8, T), jnp.int32),
            pltpu.VMEM((8, T), jnp.int32),
            pltpu.VMEM((TOP, T), jnp.int32),
            pltpu.VMEM((TOP, T), F32),
            pltpu.VMEM((VOC, T), F32),
            pltpu.VMEM((VOC, T), F32),
            pltpu.VMEM((32, 1, T), F32),
            pltpu.VMEM((VOC, T), BF),
            pltpu.VMEM((4, NZ, CH, T), BF),
            pltpu.VMEM((2, NZ, CH, T), BF),
            pltpu.VMEM((2 * NZ, CH, T), BF),
            pltpu.VMEM((2 * NZ, CH, T), BF),
            pltpu.VMEM((CH, T), F32),
            pltpu.VMEM((2, 2, 2, CH, T), BF),
            pltpu.VMEM((4 * ZX, CH, T), BF),
            pltpu.VMEM((2, 4, 2, 2, 2, CH, T), BF),
            pltpu.VMEM((2, 2, CH, T), BF),
            pltpu.VMEM((16, 16, 128), BF),
            dma((7,)),
            dma,
            dma((ZX,)),
            dma,
            dma,
            dma,
            dma,
            dma((2,)),
            dma,
            dma,
            dma,
            dma((2, 2, 2, 2, 2)),
            dma((2, 2, 2)),
            dma((2,)),
            dma,
            dma,
            dma,
            dma,
            pltpu.SemaphoreType.REGULAR,
        ],
        compiler_params=pltpu.CompilerParams(
            collective_id=0, has_side_effects=True, vmem_limit_bytes=24 * 1024 * 1024
        ),
    )(
        tile_used, *(pltpu.with_memory_space_constraint(value, pltpu.HBM) for value in given)
    )
    grad, kernel_grad, head = pl.pallas_call(
        put_out,
        out_shape=shapes,
        in_specs=[vmem] * 3,
        out_specs=(anywhere,) * 3,
        scratch_shapes=[dma((3,))],
        compiler_params=pltpu.CompilerParams(vmem_limit_bytes=4 * 1024 * 1024),
    )(*results)
    return grad.T, kernel_grad, head.reshape(2 * CH, VOC)


def solution(mesh):
    return jax.shard_map(
        local,
        mesh=mesh,
        in_specs=(
            P("dp", "mp"),
            P(None, "mp"),
            P(None, "mp"),
            P("dp", None),
            P("dp"),
            P("dp", None),
            P("dp", None),
            P("dp"),
        ),
        out_specs=(P("dp", "mp"), P(None, "mp"), P("dp", "mp")),
        check_vma=False,
    )
```

```python
import jax
import jax.numpy as jnp
from jax import lax
from jax.experimental import pallas as pl
from jax.experimental.pallas import tpu as pltpu
from jax.sharding import PartitionSpec as P

MESH = pl.DeviceIdType.MESH
TAPS = 32
LEFT = (TAPS - 1) // 2
TOP = 32
NZ = 8
NY = 8
CH = 48
T = 256
VOC = 512
ZX = 16
F32 = jnp.float32
BF = jnp.bfloat16

NEAR = (1, 7, 2, 6, 3, 5, 4)
FAR = (4, 3, 5, 2, 6, 1, 7)
SENDS = (4, 1, 7, 2, 6, 3, 5)


def eye(n):
    same = lax.broadcasted_iota(jnp.int32, (n, n), 0) == lax.broadcasted_iota(jnp.int32, (n, n), 1)
    return jnp.where(same, 1.0, 0.0).astype(BF)


def turned(values):
    return lax.dot_general(
        eye(values.shape[1]), values, (((1,), (1,)), ((), ())), preferred_element_type=F32
    )


def kernel(
    used, frames_hbm, taps_hbm, w_hbm, seg_hbm, ids_hbm, tlog_hbm, scale_hbm,
    out_in, out_k, out_h,
    frames, taps, seg, ids, tlog, scale,
    w, wt, conv, xt, xm, src_rows, dst_rows, rel_ids, teach, tgt, ex, stats, gt,
    cg, cin, xsend, xin, zsend, zin, grad,
    first, hh, rin, xrin, ky,
    in_sem, a_send, a_recv, a_core, b_send, b_recv, dc_send, dc_recv, dx_send, dx_recv, dz_send, dz_recv,
    r_send, r_recv, r4_recv, r1_recv, cx_send, cx_recv, k_send, k_recv, column_sem,
):
    m = lax.axis_index("mp")
    d = lax.axis_index("dp")
    c, xl, z = m % 2, (m // 2) % 2, m // 4
    y, xh = d % NY, d // NY
    zx = m // 2
    oc, ox, oh = 1 - c, 1 - xl, 1 - xh
    core_peer = {"mp": m + 1 - 2 * c}
    x_peer = {"mp": m + 2 - 4 * xl}
    h_peer = {"dp": oh * NY + y}

    def z_at(off):
        return (z + off) % NZ

    def z_peer(off):
        return {"mp": z_at(off) * 4 + xl * 2 + c}

    def y_at(off):
        return (y + off + NY) % NY

    def y_peer(off):
        return {"dp": xh * NY + y_at(off)}

    pairs = (
        (frames_hbm, frames), (taps_hbm, taps), (seg_hbm, seg),
        (w_hbm, w), (ids_hbm, ids), (tlog_hbm, tlog), (scale_hbm, scale),
    )
    loads = [pltpu.make_async_copy(src, dst, in_sem.at[k]) for k, (src, dst) in enumerate(pairs)]
    for load in loads:
        load.start()

    barrier = pltpu.get_barrier_semaphore()

    near = [z_peer(off) for off in FAR] + [y_peer(off) for off in FAR] + [x_peer, core_peer, h_peer]
    for peer in near:
        pl.semaphore_signal(barrier, inc=1, device_id=peer, device_id_type=MESH)

    def remote(src, dst, send, recv, peer):
        return pltpu.make_async_remote_copy(
            src_ref=src, dst_ref=dst, send_sem=send, recv_sem=recv, device_id=peer, device_id_type=MESH
        )

    for load in loads[:3]:
        load.wait()

    lane = lax.broadcasted_iota(jnp.int32, (8, T), 1)
    valid = lane < used[0]
    seg_rows = jnp.broadcast_to(seg[...], (8, T))
    src_rows[...] = jnp.where(valid, seg_rows, -1)
    dst_rows[...] = jnp.where(valid, seg_rows, -2)
    xt[...] = frames[...].astype(F32)
    tap_t = turned(taps[...])

    def kept(delta):
        rolled = src_rows[...]
        if delta:
            rolled = pltpu.roll(rolled, (-delta) % T, 1)
        keep = rolled == dst_rows[...]
        if delta > 0:
            keep = keep & (lane < T - delta)
        if delta < 0:
            keep = keep & (lane >= -delta)
        return keep

    def moved(values, delta):
        return pltpu.roll(values, (-delta) % T, 1) if delta else values

    def only(keep, values):
        return jnp.where(keep[None], values.reshape(CH // 8, 8, T), 0.0).reshape(CH, T)

    acc = jnp.zeros((CH, T), F32)
    for j in range(TAPS):
        delta = j - LEFT
        source = only(kept(delta), moved(xt[...], delta))
        xm[j] = source
        acc = acc + source * tap_t[:, j : j + 1]
    conv[c * ZX + zx] = acc.astype(BF)

    pl.semaphore_wait(barrier, len(near))
    pl.semaphore_signal(column_sem, inc=1, device_id=h_peer, device_id_type=MESH)

    def a_copy(slot, peer):
        block = conv.at[c * ZX + slot]
        return remote(block, block, a_send, a_core if peer is core_peer else a_recv.at[slot], peer)

    def a_start(slot, peer):
        a_copy(slot, peer).start()

    a_start(zx, x_peer)
    a_start(zx, core_peer)
    for off in SENDS:
        a_start(zx, z_peer(off))

    for load in loads[3:]:
        load.wait()
    for half in range(2):
        for v in range(VOC // 128):
            part = w[:, :, half, :, v * 128 : (v + 1) * 128].reshape(ZX * CH, 128)
            wt[half, v * 128 : (v + 1) * 128, :] = part.T

    rel_ids[...] = ids[...] - m * VOC
    scores = scale[...].reshape(1, T) * tlog[...].astype(F32)
    top = jnp.exp(scores - jnp.max(scores, axis=0, keepdims=True))
    teach[...] = top / jnp.sum(top, axis=0, keepdims=True)

    @pl.loop(0, VOC // 64)
    def _(part):
        first = pl.multiple_of(part * 64, 64)
        row = lax.broadcasted_iota(jnp.int32, (64, T), 0) + first
        found = jnp.zeros((64, T), F32)
        for k in range(TOP):
            found = jnp.where(row == rel_ids[k : k + 1, :], teach[k : k + 1, :], found)
        tgt[pl.ds(first, 64), :] = found

    def over(off):
        slot = z_at(off) * 2 + ox
        a_copy(slot, x_peer).wait_recv()
        a_start(slot, core_peer)

    over(0)
    for off in NEAR:
        slot = z_at(off) * 2 + xl
        a_copy(slot, z_peer(off)).wait_recv()
        a_start(slot, x_peer)
        a_start(slot, core_peer)
    for off in NEAR:
        over(off)
    def half_of(core):
        return conv[pl.ds(core * ZX, ZX)].reshape(ZX * CH, T)

    def several(ref, count, send, recv):
        some = ref.at[pl.ds(0, count)]
        return remote(some, some, send, recv, core_peer)

    logits = jnp.dot(wt[c], half_of(c), preferred_element_type=F32)
    several(conv, ZX, a_send, a_core).wait_recv()
    logits = logits + jnp.dot(wt[oc], half_of(oc), preferred_element_type=F32)

    peak = jnp.max(logits, axis=0, keepdims=True)
    raised = jnp.exp(logits - peak)
    ex[...] = raised
    own = peak + jnp.log(jnp.sum(raised, axis=0, keepdims=True))
    stats[m] = own

    def b_copy(off, slot):
        return remote(
            stats.at[slot], stats.at[slot], b_send, b_recv, {"mp": (m + off) % 32}
        )

    @pl.loop(1, 32)
    def _(off):
        b_copy(off, m).start()

    several(conv, 31, a_send, a_core).wait_send()
    several(stats, 31, b_send, b_recv).wait_recv()

    every = stats[...]
    most = jnp.max(every, axis=0)
    norm = most + jnp.log(jnp.sum(jnp.exp(every - most[None]), axis=0))
    factor = jnp.exp(peak - norm)
    live = lax.broadcasted_iota(jnp.int32, (1, T), 1) < used[0]
    gt[...] = jnp.where(live, ex[...] * factor - tgt[...], 0.0).astype(BF)

    def row_of(side, owner):
        return (oh if side == 0 else xh) * NY + owner

    def hh_at(half, col, side, owner):
        return (half * 2 + col) * ZX + row_of(side, owner)

    def r_copy(way, dist, half, side, col, owner):
        recv = r4_recv.at[way, side, col] if dist == 4 else r_recv.at[way, dist - 2, half, side, col]
        if dist == 1:
            recv = r1_recv.at[side]
        peer = y_peer(1 if way else -1)
        if dist == 1 and side == 0:
            peer = {"dp": oh * NY + y_at(1 if way else -1)}
        src = hh.at[hh_at(half, col, side, owner)]
        if dist == 4:
            src = first.at[0, half, side, col]
        if dist == 3 and half != way:
            src = first.at[1, way, side, col]
        return remote(src, rin.at[way, dist - 1, half, side, col], r_send, recv, peer)

    def r_step(dist, late):
        for side in range(2):
            for col in range(2):
                for way in range(2):
                    owner = y_at(dist if way else -dist)
                    if dist == 4:
                        r_copy(way, dist, way, side, col, owner).start()
                        continue
                    half = way if late else 1 - way
                    if dist < 3 or late:
                        row = hh_at(half, col, side, owner)
                        r_copy(way, dist + 1, half, side, col, owner).wait_recv()
                        hh[row] = (
                            hh[row].astype(F32) + rin[way, dist, half, side, col].astype(F32)
                        ).astype(BF)
                    r_copy(way, dist, half, side, col, owner).start()

    core_copies = []

    def terms_of(core, to):
        rows = jnp.concatenate([w[:, side, core].reshape(NZ * CH, VOC) for side in (ox, xl)])
        terms = jnp.dot(rows, gt[...], preferred_element_type=F32).astype(BF)
        for side in range(2):
            cg[to + side] = terms[side * NZ * CH : (side + 1) * NZ * CH].reshape(NZ, CH, T)

    terms_of(oc, 0)
    for k in range(2):
        copy = remote(cg.at[k], cin.at[k], dc_send, dc_recv.at[k], core_peer)
        copy.start()
        core_copies.append(copy)

    spots = [(half, side, 4) for half in range(2) for side in range(2)]
    spots += [(1 - way, side, 3 if way else -3) for way in range(2) for side in range(2)]
    rows = jnp.concatenate([conv[half * ZX + row_of(side, y_at(off))] for half, side, off in spots])
    for col in range(2):
        part = lax.dot_general(
            rows, gt[col * T : (col + 1) * T, :], (((1,), (1,)), ((), ())), preferred_element_type=F32
        ).astype(BF)
        for k in range(len(spots)):
            first[k // 4, k // 2 % 2, k % 2, col] = part[k * CH : (k + 1) * CH]
    r_step(4, True)

    terms_of(c, 2)

    def d_copy(i, off):
        peer = {"mp": z_at(off) * 4 + (xl if i else ox) * 2 + c}
        return remote(zsend.at[i * NZ + off], zin.at[i * NZ + off], dz_send, dz_recv, peer)

    d_near = [(i, off) for i in range(2) for off in (2, 6, 1, 7, 0) if (i, off) != (1, 0)]
    d_far = (4, 3, 5)

    def own_sum(i, at):
        return cg[2 + i, at].astype(F32) + cin[i, at].astype(F32)

    def dx_copy(k):
        return remote(xsend.at[k], xin.at[k], dx_send, dx_recv, x_peer)

    core_copies[0].wait_recv()
    for k, off in enumerate(d_far):
        xsend[k] = own_sum(0, z_at(off)).astype(BF)
        dx_copy(k).start()
    for i, off in d_near:
        if (i, off) == (1, 2):
            core_copies[1].wait_recv()
        zsend[i * NZ + off] = own_sum(i, z_at(off)).astype(BF)
        d_copy(i, off).start()
    grad[...] = own_sum(1, z)
    r_step(3, False)

    for half in range(2):
        for col in range(2):
            hh[(half * 2 + col) * ZX : (half * 2 + col + 1) * ZX] = (
                lax.dot_general(
                    half_of(half),
                    gt[col * T : (col + 1) * T, :],
                    (((1,), (1,)), ((), ())),
                    preferred_element_type=F32,
                )
                .astype(BF)
                .reshape(ZX, CH, T)
            )

    several(stats, 31, b_send, b_recv).wait_send()
    several(cg, 2, dc_send, dc_recv.at[0]).wait_send()
    r_step(3, True)
    r_step(2, False)
    several(xin, 3, dx_send, dx_recv).wait_recv()
    for k, off in enumerate(d_far):
        zsend[NZ + off] = (own_sum(1, z_at(off)) + xin[k].astype(F32)).astype(BF)
        d_copy(1, off).start()
    several(xin, 3, dx_send, dx_recv).wait_send()
    r_step(2, True)

    def cx_copy(half, col):
        return remote(
            hh.at[hh_at(half, col, 0, y)],
            xrin.at[half, col],
            cx_send,
            cx_recv,
            h_peer,
        )

    for half in range(2):
        for col in range(2):
            cx_copy(half, col).start()
    pl.semaphore_wait(column_sem, 1)
    r_step(1, False)
    conv_grad = grad[...]
    several(zin, 12, dz_send, dz_recv).wait_recv()
    for i, off in d_near + [(1, off) for off in d_far]:
        conv_grad = conv_grad + zin[i * NZ + off].astype(F32)
    grad[...] = conv_grad

    group = lax.broadcasted_iota(jnp.int32, (1, 8, 128), 2)
    packed = jnp.zeros((2, 8, 128), F32)
    for j in range(TAPS):
        terms = xm[j] * grad[...]
        sums = jnp.sum(terms[:, :128] + terms[:, 128:], axis=1, keepdims=True).reshape(CH // 8, 8, 1)
        for g in range(3):
            packed = jnp.where(group == g * TAPS + j, sums[2 * g : 2 * g + 2], packed)
    ky[d] = packed.reshape(16, 128).astype(BF)

    def k_copy(off, slot):
        return remote(ky.at[slot], ky.at[slot], k_send, k_recv, {"dp": (d + off) % 16})

    @pl.loop(1, 16)
    def _(off):
        k_copy(off, d).start()

    r_step(1, True)

    acc = jnp.zeros((CH, T), F32)
    for j in range(TAPS):
        delta = j - LEFT
        acc = acc + only(kept(-delta), moved(grad[...], -delta) * tap_t[:, j : j + 1])
    out_in[...] = acc

    several(zin, 12, dz_send, dz_recv).wait_send()
    several(hh, 4, cx_send, cx_recv).wait_send()

    several(hh, 4, cx_send, cx_recv).wait_recv()

    def y_total(half, col, total, side):
        for way in range(2):
            total = total + rin[way, 0, half, side, col].astype(F32)
        return total

    several(hh, 8, r_send, r1_recv.at[1]).wait_recv()
    for half in range(2):
        for col in range(2):
            total = hh[hh_at(half, col, 1, y)].astype(F32) + xrin[half, col].astype(F32)
            out_h[half, :, col * T : (col + 1) * T] = y_total(half, col, total, 1)

    several(ky, 15, k_send, k_recv).wait_recv()
    flat = jnp.sum(ky[...].astype(F32), axis=0).T
    out_k[...] = jnp.concatenate([flat[g * TAPS : (g + 1) * TAPS, :] for g in range(3)], axis=1)

    several(hh, 8, r_send, r1_recv.at[0]).wait_recv()
    for half in range(2):
        for col in range(2):
            cols = slice(col * T, (col + 1) * T)
            out_h[half, :, cols] = y_total(half, col, out_h[half, :, cols], 0)

    several(hh, 56, r_send, r1_recv.at[0]).wait_send()
    several(ky, 15, k_send, k_recv).wait_send()


def put_out(a, b, c, out_a, out_b, out_c, sem):
    copies = [
        pltpu.make_async_copy(src, dst, sem.at[k]) for k, (src, dst) in enumerate(((c, out_c), (a, out_a), (b, out_b)))
    ]
    for copy in copies:
        copy.start()
    for copy in copies:
        copy.wait()


def local(frames, conv_kernel, head_weight, utterance_ids, tile_used, teacher_ids, teacher_logits, teacher_scale):
    vmem = pl.BlockSpec(memory_space=pltpu.VMEM)
    anywhere = pl.BlockSpec(memory_space=pl.ANY)
    dma = pltpu.SemaphoreType.DMA
    shapes = (
        jax.ShapeDtypeStruct((CH, T), F32),
        jax.ShapeDtypeStruct((TAPS, CH), F32),
        jax.ShapeDtypeStruct((2, CH, VOC), F32),
    )
    given = (
        frames.T,
        conv_kernel,
        head_weight.reshape(NZ, 2, 2, CH, VOC),
        utterance_ids,
        teacher_ids.T,
        teacher_logits.T,
        teacher_scale,
    )
    results = pl.pallas_call(
        kernel,
        out_shape=shapes,
        in_specs=[pl.BlockSpec(memory_space=pltpu.SMEM)] + [anywhere] * 7,
        out_specs=(vmem, vmem, vmem),
        scratch_shapes=[
            pltpu.VMEM((CH, T), BF),
            pltpu.VMEM((TAPS, CH), BF),
            pltpu.VMEM((1, T), jnp.int32),
            pltpu.VMEM((TOP, T), jnp.int32),
            pltpu.VMEM((TOP, T), jnp.int32),
            pltpu.VMEM((T,), F32),
            pltpu.VMEM((NZ, 2, 2, CH, VOC), BF),
            pltpu.VMEM((2, VOC, ZX * CH), BF),
            pltpu.VMEM((2 * ZX, CH, T), BF),
            pltpu.VMEM((CH, T), F32),
            pltpu.VMEM((TAPS, CH, T), F32),
            pltpu.VMEM((8, T), jnp.int32),
            pltpu.VMEM((8, T), jnp.int32),
            pltpu.VMEM((TOP, T), jnp.int32),
            pltpu.VMEM((TOP, T), F32),
            pltpu.VMEM((VOC, T), F32),
            pltpu.VMEM((VOC, T), F32),
            pltpu.VMEM((32, 1, T), F32),
            pltpu.VMEM((VOC, T), BF),
            pltpu.VMEM((4, NZ, CH, T), BF),
            pltpu.VMEM((2, NZ, CH, T), BF),
            pltpu.VMEM((3, CH, T), BF),
            pltpu.VMEM((3, CH, T), BF),
            pltpu.VMEM((2 * NZ, CH, T), BF),
            pltpu.VMEM((2 * NZ, CH, T), BF),
            pltpu.VMEM((CH, T), F32),
            pltpu.VMEM((2, 2, 2, 2, CH, T), BF),
            pltpu.VMEM((4 * ZX, CH, T), BF),
            pltpu.VMEM((2, 4, 2, 2, 2, CH, T), BF),
            pltpu.VMEM((2, 2, CH, T), BF),
            pltpu.VMEM((16, 16, 128), BF),
            dma((7,)),
            dma,
            dma((ZX,)),
            dma,
            dma,
            dma,
            dma,
            dma((2,)),
            dma,
            dma,
            dma,
            dma,
            dma,
            dma((2, 2, 2, 2, 2)),
            dma((2, 2, 2)),
            dma((2,)),
            dma,
            dma,
            dma,
            dma,
            pltpu.SemaphoreType.REGULAR,
        ],
        compiler_params=pltpu.CompilerParams(
            collective_id=0, has_side_effects=True, vmem_limit_bytes=24 * 1024 * 1024
        ),
    )(
        tile_used, *(pltpu.with_memory_space_constraint(value, pltpu.HBM) for value in given)
    )
    grad, kernel_grad, head = pl.pallas_call(
        put_out,
        out_shape=shapes,
        in_specs=[vmem] * 3,
        out_specs=(anywhere,) * 3,
        scratch_shapes=[dma((3,))],
        compiler_params=pltpu.CompilerParams(vmem_limit_bytes=4 * 1024 * 1024),
    )(*results)
    return grad.T, kernel_grad, head.reshape(2 * CH, VOC)


def solution(mesh):
    return jax.shard_map(
        local,
        mesh=mesh,
        in_specs=(
            P("dp", "mp"),
            P(None, "mp"),
            P(None, "mp"),
            P("dp", None),
            P("dp"),
            P("dp", None),
            P("dp", None),
            P("dp"),
        ),
        out_specs=(P("dp", "mp"), P(None, "mp"), P("dp", "mp")),
        check_vma=False,
    )
```

```python
import jax
import jax.numpy as jnp
from jax import lax
from jax.experimental import pallas as pl
from jax.experimental.pallas import tpu as pltpu
from jax.sharding import PartitionSpec as P

MESH = pl.DeviceIdType.MESH
TAPS = 32
LEFT = (TAPS - 1) // 2
TOP = 32
NZ = 8
NY = 8
CH = 48
T = 256
VOC = 512
ZX = 16
F32 = jnp.float32
BF = jnp.bfloat16

NEAR = (1, 7, 2, 6, 3, 5, 4)
FAR = (4, 3, 5, 2, 6, 1, 7)
SENDS = (4, 1, 7, 2, 6, 3, 5)


def eye(n):
    same = lax.broadcasted_iota(jnp.int32, (n, n), 0) == lax.broadcasted_iota(jnp.int32, (n, n), 1)
    return jnp.where(same, 1.0, 0.0).astype(BF)


def turned(values):
    return lax.dot_general(
        eye(values.shape[1]), values, (((1,), (1,)), ((), ())), preferred_element_type=F32
    )


def kernel(
    used, frames_hbm, taps_hbm, w_hbm, seg_hbm, ids_hbm, tlog_hbm, scale_hbm,
    out_in, out_k, out_h,
    frames, taps, seg, ids, tlog, scale,
    w, wt, conv, xt, xm, src_rows, dst_rows, rel_ids, teach, tgt, ex, stats, gt,
    cg, cin, xsend, xin, zsend, zin, grad,
    first, hh, rin, xrin, ky,
    in_sem, a_send, a_recv, a_core, b_send, b_recv, dc_send, dc_recv, dx_send, dx_recv, dz_send, dz_recv,
    r_send, r_recv, r4_recv, r1_recv, cx_send, cx_recv, k_send, k_recv, column_sem,
):
    m = lax.axis_index("mp")
    d = lax.axis_index("dp")
    c, xl, z = m % 2, (m // 2) % 2, m // 4
    y, xh = d % NY, d // NY
    zx = m // 2
    oc, ox, oh = 1 - c, 1 - xl, 1 - xh
    core_peer = {"mp": m + 1 - 2 * c}
    x_peer = {"mp": m + 2 - 4 * xl}
    h_peer = {"dp": oh * NY + y}

    def z_at(off):
        return (z + off) % NZ

    def z_peer(off):
        return {"mp": z_at(off) * 4 + xl * 2 + c}

    def y_at(off):
        return (y + off + NY) % NY

    def y_peer(off):
        return {"dp": xh * NY + y_at(off)}

    pairs = (
        (frames_hbm, frames), (taps_hbm, taps), (seg_hbm, seg),
        (w_hbm, w), (ids_hbm, ids), (tlog_hbm, tlog), (scale_hbm, scale),
    )
    loads = [pltpu.make_async_copy(src, dst, in_sem.at[k]) for k, (src, dst) in enumerate(pairs)]
    for load in loads:
        load.start()

    barrier = pltpu.get_barrier_semaphore()

    near = [z_peer(off) for off in FAR] + [y_peer(off) for off in FAR] + [x_peer, core_peer, h_peer]
    for peer in near:
        pl.semaphore_signal(barrier, inc=1, device_id=peer, device_id_type=MESH)

    def remote(src, dst, send, recv, peer):
        return pltpu.make_async_remote_copy(
            src_ref=src, dst_ref=dst, send_sem=send, recv_sem=recv, device_id=peer, device_id_type=MESH
        )

    for load in loads[:3]:
        load.wait()

    lane = lax.broadcasted_iota(jnp.int32, (8, T), 1)
    valid = lane < used[0]
    seg_rows = jnp.broadcast_to(seg[...], (8, T))
    src_rows[...] = jnp.where(valid, seg_rows, -1)
    dst_rows[...] = jnp.where(valid, seg_rows, -2)
    xt[...] = frames[...].astype(F32)
    tap_t = turned(taps[...])

    def kept(delta):
        rolled = src_rows[...]
        if delta:
            rolled = pltpu.roll(rolled, (-delta) % T, 1)
        keep = rolled == dst_rows[...]
        if delta > 0:
            keep = keep & (lane < T - delta)
        if delta < 0:
            keep = keep & (lane >= -delta)
        return keep

    def moved(values, delta):
        return pltpu.roll(values, (-delta) % T, 1) if delta else values

    def only(keep, values):
        return jnp.where(keep[None], values.reshape(CH // 8, 8, T), 0.0).reshape(CH, T)

    acc = jnp.zeros((CH, T), F32)
    for j in range(TAPS):
        delta = j - LEFT
        source = only(kept(delta), moved(xt[...], delta))
        xm[j] = source
        acc = acc + source * tap_t[:, j : j + 1]
    conv[c * ZX + zx] = acc.astype(BF)

    pl.semaphore_wait(barrier, len(near))
    pl.semaphore_signal(column_sem, inc=1, device_id=h_peer, device_id_type=MESH)

    def a_copy(slot, peer):
        block = conv.at[c * ZX + slot]
        return remote(block, block, a_send, a_core if peer is core_peer else a_recv.at[slot], peer)

    def a_start(slot, peer):
        a_copy(slot, peer).start()

    a_start(zx, x_peer)
    a_start(zx, core_peer)
    for off in SENDS:
        a_start(zx, z_peer(off))

    for load in loads[3:]:
        load.wait()
    for half in range(2):
        for v in range(VOC // 128):
            part = w[:, :, half, :, v * 128 : (v + 1) * 128].reshape(ZX * CH, 128)
            wt[half, v * 128 : (v + 1) * 128, :] = part.T

    rel_ids[...] = ids[...] - m * VOC
    scores = scale[...].reshape(1, T) * tlog[...].astype(F32)
    top = jnp.exp(scores - jnp.max(scores, axis=0, keepdims=True))
    teach[...] = top / jnp.sum(top, axis=0, keepdims=True)

    @pl.loop(0, VOC // 64)
    def _(part):
        first = pl.multiple_of(part * 64, 64)
        row = lax.broadcasted_iota(jnp.int32, (64, T), 0) + first
        found = jnp.zeros((64, T), F32)
        for k in range(TOP):
            found = jnp.where(row == rel_ids[k : k + 1, :], teach[k : k + 1, :], found)
        tgt[pl.ds(first, 64), :] = found

    def over(off):
        slot = z_at(off) * 2 + ox
        a_copy(slot, x_peer).wait_recv()
        a_start(slot, core_peer)

    over(0)
    for off in NEAR:
        slot = z_at(off) * 2 + xl
        a_copy(slot, z_peer(off)).wait_recv()
        a_start(slot, x_peer)
        a_start(slot, core_peer)
    for off in NEAR:
        over(off)
    def half_of(core):
        return conv[pl.ds(core * ZX, ZX)].reshape(ZX * CH, T)

    def several(ref, count, send, recv):
        some = ref.at[pl.ds(0, count)]
        return remote(some, some, send, recv, core_peer)

    logits = jnp.dot(wt[c], half_of(c), preferred_element_type=F32)
    several(conv, ZX, a_send, a_core).wait_recv()
    logits = logits + jnp.dot(wt[oc], half_of(oc), preferred_element_type=F32)

    peak = jnp.max(logits, axis=0, keepdims=True)
    raised = jnp.exp(logits - peak)
    ex[...] = raised
    own = peak + jnp.log(jnp.sum(raised, axis=0, keepdims=True))
    stats[m] = own

    for off in (*FAR, 0):
        for side, core in ((ox, oc), (ox, c), (xl, oc), (xl, c)):
            if off or side is not xl or core is not c:
                peer = {"mp": z_at(off) * 4 + side * 2 + core}
                remote(stats.at[m], stats.at[m], b_send, b_recv, peer).start()

    several(conv, 31, a_send, a_core).wait_send()
    several(stats, 31, b_send, b_recv).wait_recv()

    every = stats[...]
    most = jnp.max(every, axis=0)
    norm = most + jnp.log(jnp.sum(jnp.exp(every - most[None]), axis=0))
    factor = jnp.exp(peak - norm)
    live = lax.broadcasted_iota(jnp.int32, (1, T), 1) < used[0]
    gt[...] = jnp.where(live, ex[...] * factor - tgt[...], 0.0).astype(BF)

    def row_of(side, owner):
        return (oh if side == 0 else xh) * NY + owner

    def hh_at(half, col, side, owner):
        return (half * 2 + col) * ZX + row_of(side, owner)

    def r_copy(way, dist, half, side, col, owner):
        recv = r4_recv.at[way, side, col] if dist == 4 else r_recv.at[way, dist - 2, half, side, col]
        if dist == 1:
            recv = r1_recv.at[side]
        peer = y_peer(1 if way else -1)
        if dist == 1 and side == 0:
            peer = {"dp": oh * NY + y_at(1 if way else -1)}
        src = hh.at[hh_at(half, col, side, owner)]
        if dist == 4:
            src = first.at[0, half, side, col]
        if dist == 3 and half != way:
            src = first.at[1, way, side, col]
        return remote(src, rin.at[way, dist - 1, half, side, col], r_send, recv, peer)

    def r_step(dist, late):
        for side in range(2):
            for col in range(2):
                for way in range(2):
                    owner = y_at(dist if way else -dist)
                    if dist == 4:
                        r_copy(way, dist, way, side, col, owner).start()
                        continue
                    half = way if late else 1 - way
                    if dist < 3 or late:
                        row = hh_at(half, col, side, owner)
                        r_copy(way, dist + 1, half, side, col, owner).wait_recv()
                        hh[row] = (
                            hh[row].astype(F32) + rin[way, dist, half, side, col].astype(F32)
                        ).astype(BF)
                    r_copy(way, dist, half, side, col, owner).start()

    core_copies = []

    def terms_of(core, to):
        rows = jnp.concatenate([w[:, side, core].reshape(NZ * CH, VOC) for side in (ox, xl)])
        terms = jnp.dot(rows, gt[...], preferred_element_type=F32).astype(BF)
        for side in range(2):
            cg[to + side] = terms[side * NZ * CH : (side + 1) * NZ * CH].reshape(NZ, CH, T)

    terms_of(oc, 0)
    for k in range(2):
        copy = remote(cg.at[k], cin.at[k], dc_send, dc_recv.at[k], core_peer)
        copy.start()
        core_copies.append(copy)

    spots = [(half, side, 4) for half in range(2) for side in range(2)]
    spots += [(1 - way, side, 3 if way else -3) for way in range(2) for side in range(2)]
    rows = jnp.concatenate([conv[half * ZX + row_of(side, y_at(off))] for half, side, off in spots])
    for col in range(2):
        part = lax.dot_general(
            rows, gt[col * T : (col + 1) * T, :], (((1,), (1,)), ((), ())), preferred_element_type=F32
        ).astype(BF)
        for k in range(len(spots)):
            first[k // 4, k // 2 % 2, k % 2, col] = part[k * CH : (k + 1) * CH]
    r_step(4, True)

    terms_of(c, 2)

    def d_copy(i, off):
        peer = {"mp": z_at(off) * 4 + (xl if i else ox) * 2 + c}
        return remote(zsend.at[i * NZ + off], zin.at[i * NZ + off], dz_send, dz_recv, peer)

    d_near = [(i, off) for i in range(2) for off in (2, 6, 1, 7, 0) if (i, off) != (1, 0)]
    d_far = (4, 3, 5)

    def own_sum(i, at):
        return cg[2 + i, at].astype(F32) + cin[i, at].astype(F32)

    def dx_copy(k):
        return remote(xsend.at[k], xin.at[k], dx_send, dx_recv, x_peer)

    core_copies[0].wait_recv()
    for k, off in enumerate(d_far):
        xsend[k] = own_sum(0, z_at(off)).astype(BF)
        dx_copy(k).start()
    for i, off in d_near:
        if (i, off) == (1, 2):
            core_copies[1].wait_recv()
        zsend[i * NZ + off] = own_sum(i, z_at(off)).astype(BF)
        d_copy(i, off).start()
    grad[...] = own_sum(1, z)
    r_step(3, False)

    for half in range(2):
        for col in range(2):
            hh[(half * 2 + col) * ZX : (half * 2 + col + 1) * ZX] = (
                lax.dot_general(
                    half_of(half),
                    gt[col * T : (col + 1) * T, :],
                    (((1,), (1,)), ((), ())),
                    preferred_element_type=F32,
                )
                .astype(BF)
                .reshape(ZX, CH, T)
            )

    several(stats, 31, b_send, b_recv).wait_send()
    several(cg, 2, dc_send, dc_recv.at[0]).wait_send()
    r_step(3, True)
    r_step(2, False)
    several(xin, 3, dx_send, dx_recv).wait_recv()
    for k, off in enumerate(d_far):
        zsend[NZ + off] = (own_sum(1, z_at(off)) + xin[k].astype(F32)).astype(BF)
        d_copy(1, off).start()
    several(xin, 3, dx_send, dx_recv).wait_send()
    r_step(2, True)

    def cx_copy(half, col):
        return remote(
            hh.at[hh_at(half, col, 0, y)],
            xrin.at[half, col],
            cx_send,
            cx_recv,
            h_peer,
        )

    for half in range(2):
        for col in range(2):
            cx_copy(half, col).start()
    pl.semaphore_wait(column_sem, 1)
    r_step(1, False)
    conv_grad = grad[...]
    several(zin, 12, dz_send, dz_recv).wait_recv()
    for i, off in d_near + [(1, off) for off in d_far]:
        conv_grad = conv_grad + zin[i * NZ + off].astype(F32)
    grad[...] = conv_grad

    group = lax.broadcasted_iota(jnp.int32, (1, 8, 128), 2)
    packed = jnp.zeros((2, 8, 128), F32)
    for j in range(TAPS):
        terms = xm[j] * grad[...]
        sums = jnp.sum(terms[:, :128] + terms[:, 128:], axis=1, keepdims=True).reshape(CH // 8, 8, 1)
        for g in range(3):
            packed = jnp.where(group == g * TAPS + j, sums[2 * g : 2 * g + 2], packed)
    ky[d] = packed.reshape(16, 128).astype(BF)

    for off in (*FAR, 0):
        for side in (oh, xh):
            if off or side is not xh:
                remote(ky.at[d], ky.at[d], k_send, k_recv, {"dp": side * NY + y_at(off)}).start()

    r_step(1, True)

    acc = jnp.zeros((CH, T), F32)
    for j in range(TAPS):
        delta = j - LEFT
        acc = acc + only(kept(-delta), moved(grad[...], -delta) * tap_t[:, j : j + 1])
    out_in[...] = acc

    several(zin, 12, dz_send, dz_recv).wait_send()
    several(hh, 4, cx_send, cx_recv).wait_send()

    several(hh, 4, cx_send, cx_recv).wait_recv()

    def y_total(half, col, total, side):
        for way in range(2):
            total = total + rin[way, 0, half, side, col].astype(F32)
        return total

    several(hh, 8, r_send, r1_recv.at[1]).wait_recv()
    for half in range(2):
        for col in range(2):
            total = hh[hh_at(half, col, 1, y)].astype(F32) + xrin[half, col].astype(F32)
            out_h[half, :, col * T : (col + 1) * T] = y_total(half, col, total, 1)

    several(ky, 15, k_send, k_recv).wait_recv()
    flat = jnp.sum(ky[...].astype(F32), axis=0).T
    out_k[...] = jnp.concatenate([flat[g * TAPS : (g + 1) * TAPS, :] for g in range(3)], axis=1)

    several(hh, 8, r_send, r1_recv.at[0]).wait_recv()
    for half in range(2):
        for col in range(2):
            cols = slice(col * T, (col + 1) * T)
            out_h[half, :, cols] = y_total(half, col, out_h[half, :, cols], 0)

    several(hh, 56, r_send, r1_recv.at[0]).wait_send()
    several(ky, 15, k_send, k_recv).wait_send()


def put_out(a, b, c, out_a, out_b, out_c, sem):
    copies = [
        pltpu.make_async_copy(src, dst, sem.at[k]) for k, (src, dst) in enumerate(((c, out_c), (a, out_a), (b, out_b)))
    ]
    for copy in copies:
        copy.start()
    for copy in copies:
        copy.wait()


def local(frames, conv_kernel, head_weight, utterance_ids, tile_used, teacher_ids, teacher_logits, teacher_scale):
    vmem = pl.BlockSpec(memory_space=pltpu.VMEM)
    anywhere = pl.BlockSpec(memory_space=pl.ANY)
    dma = pltpu.SemaphoreType.DMA
    shapes = (
        jax.ShapeDtypeStruct((CH, T), F32),
        jax.ShapeDtypeStruct((TAPS, CH), F32),
        jax.ShapeDtypeStruct((2, CH, VOC), F32),
    )
    given = (
        frames.T,
        conv_kernel,
        head_weight.reshape(NZ, 2, 2, CH, VOC),
        utterance_ids,
        teacher_ids.T,
        teacher_logits.T,
        teacher_scale,
    )
    results = pl.pallas_call(
        kernel,
        out_shape=shapes,
        in_specs=[pl.BlockSpec(memory_space=pltpu.SMEM)] + [anywhere] * 7,
        out_specs=(vmem, vmem, vmem),
        scratch_shapes=[
            pltpu.VMEM((CH, T), BF),
            pltpu.VMEM((TAPS, CH), BF),
            pltpu.VMEM((1, T), jnp.int32),
            pltpu.VMEM((TOP, T), jnp.int32),
            pltpu.VMEM((TOP, T), jnp.int32),
            pltpu.VMEM((T,), F32),
            pltpu.VMEM((NZ, 2, 2, CH, VOC), BF),
            pltpu.VMEM((2, VOC, ZX * CH), BF),
            pltpu.VMEM((2 * ZX, CH, T), BF),
            pltpu.VMEM((CH, T), F32),
            pltpu.VMEM((TAPS, CH, T), F32),
            pltpu.VMEM((8, T), jnp.int32),
            pltpu.VMEM((8, T), jnp.int32),
            pltpu.VMEM((TOP, T), jnp.int32),
            pltpu.VMEM((TOP, T), F32),
            pltpu.VMEM((VOC, T), F32),
            pltpu.VMEM((VOC, T), F32),
            pltpu.VMEM((32, 1, T), F32),
            pltpu.VMEM((VOC, T), BF),
            pltpu.VMEM((4, NZ, CH, T), BF),
            pltpu.VMEM((2, NZ, CH, T), BF),
            pltpu.VMEM((3, CH, T), BF),
            pltpu.VMEM((3, CH, T), BF),
            pltpu.VMEM((2 * NZ, CH, T), BF),
            pltpu.VMEM((2 * NZ, CH, T), BF),
            pltpu.VMEM((CH, T), F32),
            pltpu.VMEM((2, 2, 2, 2, CH, T), BF),
            pltpu.VMEM((4 * ZX, CH, T), BF),
            pltpu.VMEM((2, 4, 2, 2, 2, CH, T), BF),
            pltpu.VMEM((2, 2, CH, T), BF),
            pltpu.VMEM((16, 16, 128), BF),
            dma((7,)),
            dma,
            dma((ZX,)),
            dma,
            dma,
            dma,
            dma,
            dma((2,)),
            dma,
            dma,
            dma,
            dma,
            dma,
            dma((2, 2, 2, 2, 2)),
            dma((2, 2, 2)),
            dma((2,)),
            dma,
            dma,
            dma,
            dma,
            pltpu.SemaphoreType.REGULAR,
        ],
        compiler_params=pltpu.CompilerParams(
            collective_id=0, has_side_effects=True, vmem_limit_bytes=24 * 1024 * 1024
        ),
    )(
        tile_used, *(pltpu.with_memory_space_constraint(value, pltpu.HBM) for value in given)
    )
    grad, kernel_grad, head = pl.pallas_call(
        put_out,
        out_shape=shapes,
        in_specs=[vmem] * 3,
        out_specs=(anywhere,) * 3,
        scratch_shapes=[dma((3,))],
        compiler_params=pltpu.CompilerParams(vmem_limit_bytes=4 * 1024 * 1024),
    )(*results)
    return grad.T, kernel_grad, head.reshape(2 * CH, VOC)


def solution(mesh):
    return jax.shard_map(
        local,
        mesh=mesh,
        in_specs=(
            P("dp", "mp"),
            P(None, "mp"),
            P(None, "mp"),
            P("dp", None),
            P("dp"),
            P("dp", None),
            P("dp", None),
            P("dp"),
        ),
        out_specs=(P("dp", "mp"), P(None, "mp"), P("dp", "mp")),
        check_vma=False,
    )
```
